32 devices in a mesh: dp: 4 (over z), seq: 2 (over y), tensor: 4 (over x, core).
Axes of the slice: x: 2, y: 2, z: 4, core: 2. Of those that a mesh axis runs over, the one named last changes fastest.
Arguments:
- patch_states: bfloat16 [4, 768, 4096], P('dp', 'seq', 'tensor'), may hold values from -6 to 6
- residual_grad: bfloat16 [4, 768, 4096], P('dp', 'seq', 'tensor'), may hold values from -3 to 3
- upstream_value: bfloat16 [4, 768, 512], P('dp', 'seq'), may hold values from -6 to 6
- norm_gain: bfloat16 [4096], P('tensor'), may hold values from 0.099609375 to 1.8984375
- value_weight: bfloat16 [512, 4096], P(('dp', 'seq'), 'tensor'), may hold values from -0.09375 to 0.09375
- out_weight: bfloat16 [512, 4096], P(('dp', 'seq'), 'tensor'), may hold values from -0.25 to 0.25
- attn_out: bfloat16 [4, 768, 512], P('dp', 'seq'), may hold values from -6 to 6
- queries: bfloat16 [4, 768, 512], P('dp', 'seq', 'tensor'), may hold values from -1.5 to 1.5
- byte_keys: bfloat16 [4, 16384, 512], P('dp', 'seq', 'tensor'), may hold values from -1.5 to 1.5
- byte_values: bfloat16 [4, 16384, 512], P('dp', 'seq', 'tensor'), may hold values from -6 to 6
- patch_starts: int32 [4, 768], P('dp'), may hold values from 0 to 16383, as said below
Outputs:
- wgrad_value: float32 [512, 4096], P(('dp', 'seq'), 'tensor')
- wgrad_out: float32 [512, 4096], P(('dp', 'seq'), 'tensor')
- grad_keys: bfloat16 [4, 16384, 512], P('dp', 'seq', 'tensor')
- grad_values: bfloat16 [4, 16384, 512], P('dp', 'seq', 'tensor')
The draws below stay inside these ranges and needn't reach their ends.
Inputs may be any that keep to these rules, and one draw needn't show every extreme that they name: `patch_starts`: row i lists, increasing, the first byte of each of the 768 patches of sequence i. Every multiple of 8192 is among them, so no patch crosses the boundary between two byte shards. In every sequence one byte shard holds 768 patches, or 767 where that is fewer, and no byte shard holds more. The bytes of patch j lie on byte shard j // 384 - 1, j // 384 or j // 384 + 1.
All inputs are finite; a program needn't handle non-finite values.
Results may differ from the reference program's by a relative error of at most 0.0058.
Values may be sent and summed in bfloat16 or wider, within the bound.
A program may use at most 128 MiB of HBM per device.

```python
import math
import jax
import jax.numpy as jnp
from jax import lax

D = 4096
KVW = 512
DLW = 512
HD = 128
SEQ_LEN = 16384
PATCH_DEV = 384
SEQS = 4
NPS = 768
BYTE_DEV = 8192
N_SEQ = 2


def draw_patch_starts(key, part):

    def one_sequence(seq_key):
        heavy_key, weight_key, cut_key = jax.random.split(seq_key, 3)
        shard_ids = jnp.arange(N_SEQ, dtype=jnp.int32)
        heavy_shard = jax.random.randint(heavy_key, (), 0, N_SEQ)
        heavy_count = min(2 * PATCH_DEV, NPS - N_SEQ + 1)
        others_total = NPS - heavy_count
        short_total = (N_SEQ - 1) * PATCH_DEV - others_total
        others = (shard_ids != heavy_shard).astype(jnp.int32)
        weights = jax.random.randint(weight_key, (N_SEQ,), 1, 5) * others
        weight_total = jnp.sum(weights)
        shortfall = short_total * weights // weight_total
        deficit = short_total - jnp.sum(shortfall)
        ranking = jnp.cumsum(others) - 1
        shortfall = shortfall + ((ranking < deficit) & (others == 1)).astype(jnp.int32)
        counts = jnp.where(others == 1, PATCH_DEV - shortfall, heavy_count)
        cut_keys = jax.random.split(cut_key, N_SEQ)
        orders = jax.vmap(lambda one_key: jax.random.permutation(one_key, BYTE_DEV - 1))(cut_keys)
        chosen = (jnp.arange(BYTE_DEV - 1, dtype=jnp.int32)[None, :] < counts[:, None] - 1).astype(jnp.int32)
        marks = jnp.zeros((N_SEQ, BYTE_DEV), jnp.int32)
        marks = marks.at[shard_ids[:, None], orders + 1].set(chosen)
        marks = marks.at[:, 0].set(1)
        return jnp.nonzero(marks.reshape(-1), size=NPS)[0].astype(jnp.int32)
    seq_keys = jax.random.split(key, SEQS)
    return jax.vmap(one_sequence)(seq_keys)


def level_of(own_key, shape, cuts, low, top_value):
    gain, own = 1.0, jax.random.fold_in(own_key, 6)
    for dim, blocks in cuts:
        heights = jnp.exp(jax.random.uniform(jax.random.fold_in(own, dim), (blocks,), jnp.float32, low / len(cuts), top_value / len(cuts)))
        gain = gain * jnp.repeat(heights, shape[dim] // blocks).reshape([-1 if axis == dim else 1 for axis in range(len(shape))])
    return gain


def centred(rng, dims, spread, most, cuts=(), kind=jnp.bfloat16):
    values = jax.random.normal(rng, dims, jnp.float32) * spread
    if len(cuts) > 0:
        values = level_of(rng, dims, cuts, -0.22, 0.18) * values
    return jnp.clip(values, min=-most, max=most).astype(kind)


def setup_inputs(seed: int = 0) -> dict:
    key_list = jax.random.split(jax.random.key(seed), 12)
    patch_states = centred(key_list[0], (SEQS, NPS, D), 1.0, 6.0, ((0, 4), (1, 2), (2, 4)))
    residual_grad = centred(key_list[1], (SEQS, NPS, D), 0.5, 3.0, ((0, 4), (1, 2), (2, 4)))
    upstream_value = centred(key_list[2], (SEQS, NPS, KVW), 1.0, 6.0, ((0, 4), (1, 2)))
    norm_gain = jnp.clip(1.0 + 0.18 * jax.random.normal(key_list[3], (D,), jnp.float32), 0.099609375, 1.8984375).astype(jnp.bfloat16)
    value_weight = centred(key_list[4], (KVW, D), D ** -0.5, 0.09375, ((0, 8), (1, 4)))
    out_weight = centred(key_list[5], (DLW, D), DLW ** -0.5, 0.25, ((0, 8), (1, 4)))
    attn_out = centred(key_list[6], (SEQS, NPS, DLW), 1.0, 6.0, ((0, 4), (1, 2)))
    queries = jnp.clip(jax.random.uniform(key_list[7], (SEQS, NPS, DLW), jnp.float32, -1.5, 1.5) * level_of(key_list[7], (SEQS, NPS, DLW), ((0, 4), (1, 2), (2, 4)), -0.4, 0.0), -1.5, 1.5).astype(jnp.bfloat16)
    byte_keys = jnp.clip(jax.random.uniform(key_list[8], (SEQS, SEQ_LEN, DLW), jnp.float32, -1.5, 1.5) * level_of(key_list[8], (SEQS, SEQ_LEN, DLW), ((0, 4), (1, 2), (2, 4)), -0.4, 0.0), -1.5, 1.5).astype(jnp.bfloat16)
    byte_values = centred(key_list[9], (SEQS, SEQ_LEN, DLW), 1.0, 6.0, ((0, 4), (1, 2), (2, 4)))
    patch_starts = draw_patch_starts(jax.random.fold_in(key_list[11], 71), 0)
    return dict(patch_states=patch_states, residual_grad=residual_grad, upstream_value=upstream_value, norm_gain=norm_gain, value_weight=value_weight, out_weight=out_weight, attn_out=attn_out, queries=queries, byte_keys=byte_keys, byte_values=byte_values, patch_starts=patch_starts)


def cross_backward(query_rows, grad_rows, keys, values, segment_ids, count):
    nbytes = keys.shape[0]
    heads = keys.shape[1] // HD
    scale = 1.0 / math.sqrt(HD)
    query_f = query_rows.astype(jnp.float32).reshape(nbytes, heads, HD)
    grad_f = grad_rows.astype(jnp.float32).reshape(nbytes, heads, HD)
    keys_f = keys.astype(jnp.float32).reshape(nbytes, heads, HD)
    values_f = values.astype(jnp.float32).reshape(nbytes, heads, HD)
    scores = lax.optimization_barrier(jnp.sum(query_f * keys_f, axis=-1)) * scale
    expo = jnp.exp(scores)
    totals = jax.ops.segment_sum(expo, segment_ids, num_segments=count)
    probs = expo / totals[segment_ids]
    grad_values = (probs[..., None] * grad_f).reshape(nbytes, heads * HD).astype(jnp.bfloat16)
    prob_grad = lax.optimization_barrier(jnp.sum(grad_f * values_f, axis=-1))
    mass = jax.ops.segment_sum(probs * prob_grad, segment_ids, num_segments=count)
    score_grad = probs * (prob_grad - mass[segment_ids])
    grad_keys = (score_grad[..., None] * query_f * scale).reshape(nbytes, heads * HD).astype(jnp.bfloat16)
    return (grad_keys, grad_values)

def reference(patch_states, residual_grad, upstream_value, norm_gain, value_weight, out_weight, attn_out, queries, byte_keys, byte_values, patch_starts):
    states32 = patch_states.reshape(-1, D).astype(jnp.float32)
    gain32 = norm_gain.astype(jnp.float32)
    inv_rms = lax.rsqrt(lax.optimization_barrier(jnp.mean(states32 * states32, axis=1)) + 1e-05)
    normed = (states32 * inv_rms[:, None] * gain32).astype(jnp.bfloat16)
    upstream = upstream_value.reshape(-1, KVW)
    grad_normed = jnp.dot(upstream, value_weight, preferred_element_type=jnp.float32)
    wgrad_value = lax.dot_general(upstream, normed, (((0,), (0,)), ((), ())), preferred_element_type=jnp.float32)
    cross_sum = lax.optimization_barrier(jnp.sum(grad_normed * gain32 * states32, axis=1))
    grad_patch = (residual_grad.reshape(-1, D).astype(jnp.float32) + inv_rms[:, None] * gain32 * grad_normed - (inv_rms ** 3)[:, None] * states32 * (cross_sum / D)[:, None]).astype(jnp.bfloat16)
    wgrad_out = lax.dot_general(attn_out.reshape(-1, DLW), grad_patch, (((0,), (0,)), ((), ())), preferred_element_type=jnp.float32)
    grad_attn = lax.dot_general(grad_patch, out_weight, (((1,), (1,)), ((), ())), preferred_element_type=jnp.float32)
    grad_attn = grad_attn.astype(jnp.bfloat16).reshape(SEQS, NPS, DLW)

    def one_sequence(item):
        starts, grad_rows, query_rows, keys, values = item
        positions = jnp.arange(SEQ_LEN, dtype=jnp.int32)
        patch_index = (jnp.searchsorted(starts, positions, side='right') - 1).astype(jnp.int32)
        return cross_backward(query_rows[patch_index], grad_rows[patch_index], keys, values, patch_index, NPS)
    grad_keys, grad_values = lax.map(one_sequence, (patch_starts, grad_attn, queries, byte_keys, byte_values))
    return (wgrad_value, wgrad_out, grad_keys, grad_values)
```

```python
import functools
import math

import jax
import jax.numpy as jnp
from jax import lax
from jax.experimental import pallas as pl
from jax.experimental.pallas import tpu as pltpu
from jax.sharding import PartitionSpec as P

HD = 128


def member_sum(member32, terms):
    return lax.dot_general(
        member32,
        terms,
        (((0,), (0,)), ((), ())),
        precision=lax.Precision.HIGHEST,
        preferred_element_type=jnp.float32,
    )


def member_spread(member32, totals):
    return jnp.dot(
        member32, totals, precision=lax.Precision.HIGHEST, preferred_element_type=jnp.float32
    )


def cross_backward(member, segment_rows, keys, values, head_width):
    nbytes = keys.shape[0]
    heads = keys.shape[1] // HD
    scale = 1.0 / math.sqrt(HD)
    member32 = member.astype(jnp.float32)
    picked = jnp.dot(member, segment_rows, preferred_element_type=jnp.float32).astype(jnp.bfloat16)
    grad_f = picked[:, :head_width].astype(jnp.float32).reshape(nbytes, heads, HD)
    query_f = picked[:, head_width:].astype(jnp.float32).reshape(nbytes, heads, HD)
    keys_f = keys.astype(jnp.float32).reshape(nbytes, heads, HD)
    values_f = values.astype(jnp.float32).reshape(nbytes, heads, HD)
    scores = jnp.sum(query_f * keys_f, axis=-1) * scale
    expo = jnp.exp(scores)
    totals = member_spread(member32, member_sum(member32, expo))
    probs = expo / totals
    grad_values = (probs[..., None] * grad_f).reshape(nbytes, heads * HD).astype(jnp.bfloat16)
    prob_grad = jnp.sum(grad_f * values_f, axis=-1)
    mass = member_spread(member32, member_sum(member32, probs * prob_grad))
    score_grad = probs * (prob_grad - mass)
    grad_keys = (
        (score_grad[..., None] * query_f * scale).reshape(nbytes, heads * HD).astype(jnp.bfloat16)
    )
    return (grad_keys, grad_values)


def contract_rows(left, right):
    return lax.dot_general(
        left, right, (((0,), (0,)), ((), ())), preferred_element_type=jnp.float32
    )


def on_device(
    patch_states,
    residual_grad,
    upstream_value,
    norm_gain,
    value_weight,
    out_weight,
    attn_out,
    queries,
    byte_keys,
    byte_values,
    patch_starts,
):
    states = patch_states[0]
    patches = states.shape[0]
    width_local = states.shape[1]
    model_width = width_local * lax.axis_size("tensor")
    states32 = states.astype(jnp.float32)
    gain32 = norm_gain.astype(jnp.float32)
    upstream = upstream_value[0]
    context = attn_out[0]
    value_full, out_full = (
        lax.all_gather(value_weight, ("dp", "seq"), axis=0, tiled=True),
        lax.all_gather(out_weight, ("dp", "seq"), axis=0, tiled=True),
    )
    grad_normed = jnp.dot(upstream, value_full, preferred_element_type=jnp.float32)
    square_part = jnp.sum(states32 * states32, axis=1)
    cross_part = jnp.sum(grad_normed * gain32 * states32, axis=1)
    square_sum, cross_sum = lax.psum((square_part, cross_part), "tensor")
    inv_rms = lax.rsqrt(square_sum / model_width + 1e-05)
    normed = (states32 * inv_rms[:, None] * gain32).astype(jnp.bfloat16)
    grad_patch = (
        residual_grad[0].astype(jnp.float32)
        + inv_rms[:, None] * gain32 * grad_normed
        - (inv_rms**3)[:, None] * states32 * (cross_sum / model_width)[:, None]
    ).astype(jnp.bfloat16)
    partial_attn = lax.dot_general(
        grad_patch, out_full, (((1,), (1,)), ((), ())), preferred_element_type=jnp.float32
    )
    columns = upstream
    wgrad_value = lax.psum_scatter(
        contract_rows(columns, normed), ("dp", "seq"), scatter_dimension=0, tiled=True
    )
    columns = context
    wgrad_out = lax.psum_scatter(
        contract_rows(columns, grad_patch), ("dp", "seq"), scatter_dimension=0, tiled=True
    )
    attn_all = lax.psum(partial_attn, "tensor").astype(jnp.bfloat16)
    head_width = queries.shape[2]
    grad_attn = lax.dynamic_slice_in_dim(
        attn_all, lax.axis_index("tensor") * head_width, head_width, 1
    )
    starts = patch_starts[0]
    total_patches = starts.shape[0]
    seq_count = lax.axis_size("seq")
    seq_pos = lax.axis_index("seq")
    byte_count = byte_keys.shape[1]
    window_len = 2 * patches
    owners = starts // byte_count
    shard_ids = jnp.arange(seq_count, dtype=jnp.int32)
    firsts = jnp.sum((owners[None, :] < shard_ids[:, None]).astype(jnp.int32), axis=1)
    my_first = jnp.sum(firsts * (shard_ids == seq_pos).astype(jnp.int32))
    payload = jnp.concatenate([grad_attn, queries[0]], axis=1)
    padded_starts = jnp.concatenate(
        [starts, jnp.full((window_len,), 2 * total_patches * byte_count + byte_count, jnp.int32)]
    )
    local_starts = lax.dynamic_slice_in_dim(padded_starts, my_first, window_len)
    positions = seq_pos * byte_count + jnp.arange(byte_count, dtype=jnp.int32)
    reached = local_starts[None, :] <= positions[:, None]
    after = jnp.concatenate([reached[:, 1:], jnp.zeros((byte_count, 1), bool)], axis=1)
    member = (reached & jnp.logical_not(after)).astype(jnp.bfloat16)
    mine = seq_pos * patches + jnp.arange(patches, dtype=jnp.int32)
    targets = lax.dynamic_slice_in_dim(owners, seq_pos * patches, patches)
    target_first = jnp.sum((owners[None, :] < targets[:, None]).astype(jnp.int32), axis=1)
    slots = mine - jnp.maximum(seq_pos * patches, target_first)
    dest = targets * patches + slots
    place = (jnp.arange(seq_count * patches, dtype=jnp.int32)[:, None] == dest[None, :]).astype(
        jnp.bfloat16
    )
    outgoing = jnp.dot(place, payload, preferred_element_type=jnp.float32).astype(jnp.bfloat16)
    outgoing = outgoing.reshape(seq_count, patches, 2 * head_width)
    incoming = lax.all_to_all(outgoing, "seq", split_axis=0, concat_axis=0, tiled=True)
    wanted = my_first + jnp.arange(window_len, dtype=jnp.int32)
    sources = wanted // patches
    received_row = sources * patches + wanted - jnp.maximum(sources * patches, my_first)
    select = (
        received_row[:, None] == jnp.arange(seq_count * patches, dtype=jnp.int32)[None, :]
    ).astype(jnp.bfloat16)
    segment_rows = jnp.dot(
        select,
        incoming.reshape(seq_count * patches, 2 * head_width),
        preferred_element_type=jnp.float32,
    ).astype(jnp.bfloat16)
    grad_keys, grad_values = cross_backward(
        member, segment_rows, byte_keys[0], byte_values[0], head_width
    )
    return (wgrad_value, wgrad_out, grad_keys[None], grad_values[None])


BLK = 256
WIN = 128


def grad_kernel(
    ndp, nt, nbytes, states_in, resid_in, up_in, gain_in, vw, ow, ctx_in, q_in, starts,
    wgv, wgo, g_out, q_out, tab, bounds,
    states, resid, up, ctx, gain, wall, sqs, sqr, part, acc, rbv, lbv, ysv, yrv, rbo, lbo, yso, yro,
    pas, par, gn, nrm, gpat, trans_v, trans_o, gsend, gboth, qboth,
    s_in, s_own, s_out, s_ag, r_ag, s_sq, r_sq, s_rv, r_rv, s_lv, r_lv, s_ro, r_ro, s_lo, r_lo,
    s_yo, r_yo, s_yv, r_yv, s_pa, r_pa, s_g, r_g,
):
    dp, sq, tn = lax.axis_index("dp"), lax.axis_index("seq"), lax.axis_index("tensor")
    patches, width = states.shape
    model = width * nt
    last = ndp - 1
    mine = dp * 2 + sq
    tall = 128
    nrow = patches // tall
    ncol = width // 256

    right, left = (dp + 1, sq, tn), (dp - 1, sq, tn)
    ydev = (dp, 1 - sq, tn)

    def tdev(k):
        return (dp, sq, lax.rem(tn + k, nt))

    def copy(src, dst, ssem, rsem, dev):
        return pltpu.make_async_remote_copy(
            src_ref=src, dst_ref=dst, send_sem=ssem, recv_sem=rsem,
            device_id=dev, device_id_type=pl.DeviceIdType.MESH,
        )

    local = {}
    for i, (name, src, dst) in enumerate(
        (("states", states_in, states), ("up", up_in, up), ("resid", resid_in, resid),
         ("ctx", ctx_in, ctx), ("q", q_in, qboth.at[sq]), ("vw", vw, wall.at[0, mine]),
         ("ow", ow, wall.at[1, mine]))
    ):
        local[name] = pltpu.make_async_copy(src, dst, s_in.at[i])
        local[name].start()

    barrier = pltpu.get_barrier_semaphore()
    peers = [(lax.rem(dp + k, ndp), sq, tn) for k in range(1, ndp)]
    peers += [tdev(k) for k in range(1, nt)] + [ydev]
    for dev in peers:
        pl.semaphore_signal(barrier, inc=1, device_id=dev, device_id_type=pl.DeviceIdType.MESH)
    pl.semaphore_wait(barrier, len(peers))

    sent = []

    def go(c, cond=None):
        if cond is None:
            c.start()
        else:
            pl.when(cond)(c.start)
        sent.append((c, cond))
        return c

    weights = (vw, ow)

    def shard(w, zz, yy, dev, k, own=False):
        slot = zz * 2 + yy
        src = weights[w] if own else wall.at[w, slot]
        return copy(src, wall.at[w, slot], s_ag.at[w, k], r_ag.at[w, slot], dev)

    def ag_own_z(w):
        go(shard(w, dp, sq, right, 0, True), dp < last)
        go(shard(w, dp, sq, left, 1, True), dp > 0)

    def ag_own_y(w):
        go(shard(w, dp, sq, ydev, 2, True))

    def ag_forward(w, s):
        for zz, here, dev, onward, k in (
            (dp - s, dp - s >= 0, right, dp < last, 3 * s),
            (dp + s, dp + s <= last, left, dp > 0, 3 * ndp + 3 * s),
        ):
            pl.when(here)(shard(w, zz, sq, dev, k).wait_recv)
            go(shard(w, zz, sq, dev, k), here & onward)
            go(shard(w, zz, sq, ydev, k + 1), here)

    def ag_wait_y(w):
        for zz in range(ndp):
            shard(w, zz, 1 - sq, ydev, 2).wait_recv()

    def row_loop(fn):
        def body(i, _):
            fn(pl.ds(pl.multiple_of(i * tall, tall), tall), i)
            return 0

        lax.fori_loop(0, nrow, body, 0)

    def to_row(col):
        return jnp.broadcast_to(col, (tall, 128)).T[:8]

    def share(which):
        return [
            go(copy(sqs.at[which], sqr.at[which, k - 1], s_sq.at[which, k - 1],
                    r_sq.at[which, k - 1], tdev(k)))
            for k in range(1, nt)
        ]

    def total_col(which, i):
        rows = sqs[which, i]
        for k in range(nt - 1):
            rows = rows + sqr[which, k, i]
        return jnp.broadcast_to(rows[0:1, :], (128, tall)).T[:, 0:1]

    def inverse(i):
        return lax.rsqrt(total_col(0, i) / model + 1e-05)

    def square(here, i):
        x = states[here, :].astype(jnp.float32)
        sqs[0, i] = to_row(jnp.sum(x * x, axis=1, keepdims=True))

    def normalise(here, i):
        x = states[here, :].astype(jnp.float32)
        nrm[here, :] = (x * inverse(i) * gain[0:1, :]).astype(jnp.bfloat16)

    def wgrad(w, trans, factor):
        nblk, rows_per = part.shape[1], part.shape[2]

        def body(c, _):
            cols = pl.ds(pl.multiple_of(c * 256, 256), 256)
            out = jnp.dot(trans[...], factor[:, cols], preferred_element_type=jnp.float32)
            part[w, :, :, cols] = out.reshape(nblk, rows_per, 256)
            return 0

        lax.fori_loop(0, ncol, body, 0)

    def two(zz):
        return part[0, pl.ds(zz * 2, 2)]

    def one(zz):
        yo(zz).wait_recv()
        return part[1, zz * 2 + sq] + yro[zz].astype(jnp.float32)

    def line(d, get, buf_r, buf_l, s_r, r_r, s_l, r_l):
        for zz, valid, dev, fed, buf, ss, rs in (
            (dp + d, dp + d <= last, right, dp > 0, buf_r, s_r, r_r),
            (dp - d, dp - d >= 0, left, dp < last, buf_l, s_l, r_l),
        ):
            c = copy(buf.at[zz], buf.at[zz], ss.at[d - 1], rs.at[zz], dev)

            @pl.when(valid)
            def _(zz=zz, fed=fed, buf=buf, c=c):
                mine_part = get(zz)

                @pl.when(fed)
                def _():
                    c.wait_recv()
                    buf[zz] = (mine_part + buf[zz].astype(jnp.float32)).astype(jnp.bfloat16)

                @pl.when(jnp.logical_not(fed))
                def _():
                    buf[zz] = mine_part.astype(jnp.bfloat16)

            go(c, valid)

    def line_end(rows, buf_r, buf_l, s_r, r_r, s_l, r_l):
        for fed, dev, buf, ss, rs in (
            (dp > 0, right, buf_r, s_r, r_r),
            (dp < last, left, buf_l, s_l, r_l),
        ):
            c = copy(buf.at[dp], buf.at[dp], ss.at[0], rs.at[dp], dev)

            @pl.when(fed)
            def _(c=c, buf=buf):
                c.wait_recv()
                acc[rows] += buf[dp].astype(jnp.float32)

    line_v = (rbv, lbv, s_rv, r_rv, s_lv, r_lv)
    line_o = (rbo, lbo, s_ro, r_ro, s_lo, r_lo)

    def yo(zz):
        return copy(yso.at[zz], yro.at[zz], s_yo.at[zz], r_yo.at[zz], ydev)

    def send_yo(zz, cond=None):
        def fill():
            yso[zz] = part[1, zz * 2 + (1 - sq)].astype(jnp.bfloat16)

        fill() if cond is None else pl.when(cond)(fill)
        go(yo(zz), cond)

    ag_own_z(0)
    ag_own_y(0)
    for i in range(width // 128):
        gain[:, i * 128 : (i + 1) * 128] = jnp.broadcast_to(
            gain_in[i : i + 1, :].astype(jnp.float32), (8, 128)
        )
    local["states"].wait()
    row_loop(square)
    sq_copies = share(0)
    local["up"].wait()
    trans_v[...] = up[...].T

    first = starts[0:1, :] - sq * nbytes
    row8 = jnp.broadcast_to(first, (8, first.shape[1]))
    lane = lax.broadcasted_iota(jnp.int32, row8.shape, 1)
    after = jnp.where(
        lane == first.shape[1] - 1, 2 * nbytes, pltpu.roll(row8, first.shape[1] - 1, 1)
    )
    far = jnp.full((1, WIN), 4 * nbytes, jnp.int32)
    bounds[0:1, : first.shape[1]] = first
    bounds[1:2, : first.shape[1]] = after[0:1, :]
    bounds[0:1, first.shape[1] :] = far
    bounds[1:2, first.shape[1] :] = far

    ag_forward(0, 1)
    for c in sq_copies:
        c.wait_recv()
    row_loop(normalise)
    wgrad(0, trans_v, nrm)
    line(3, two, *line_v)

    nblocks = nbytes // BLK
    ends = lax.broadcasted_iota(jnp.int32, (nblocks, first.shape[1]), 0) * BLK + (BLK - 1)
    reach = (jnp.broadcast_to(first, ends.shape) <= ends).astype(jnp.int32)
    high = (jnp.sum(reach, axis=1, keepdims=True) - 1) // WIN
    low = (jnp.sum((first <= 0).astype(jnp.int32), axis=1, keepdims=True) - 1) // WIN
    step = lax.broadcasted_iota(jnp.int32, (nblocks, 128), 0) + high - low
    pair = lax.broadcasted_iota(jnp.int32, (nblocks, 128), 1)
    block_of = jnp.sum((step < pair).astype(jnp.int32), axis=0, keepdims=True)
    window = lax.broadcasted_iota(jnp.int32, (1, 128), 1) - block_of + low
    done = block_of >= nblocks
    tab[0:1, :] = jnp.where(done, nblocks - 1, block_of)
    tab[1:2, :] = jnp.where(done, first.shape[1] // WIN, window)

    ag_forward(0, 2)
    ag_own_z(1)
    ag_forward(0, 3)
    ag_own_y(1)
    local["ctx"].wait()
    trans_o[...] = ctx[...].T
    line(2, two, *line_v)
    ag_forward(1, 1)
    local["vw"].wait()
    ag_wait_y(0)

    def project(here, i):
        full = wall[0].reshape(up.shape[1], width)
        g = jnp.dot(up[here, :], full, preferred_element_type=jnp.float32)
        gn[here, :] = g
        x = states[here, :].astype(jnp.float32)
        sqs[1, i] = to_row(jnp.sum(g * gain[0:1, :] * x, axis=1, keepdims=True))

    row_loop(project)
    cr_copies = share(1)
    ag_forward(1, 2)
    line(1, two, *line_v)
    local["resid"].wait()
    for c in cr_copies:
        c.wait_recv()

    def make_grad(here, i):
        inv = inverse(i)
        cross = total_col(1, i) / model
        x = states[here, :].astype(jnp.float32)
        gpat[here, :] = (
            resid[here, :].astype(jnp.float32)
            + inv * gain[0:1, :] * gn[here, :]
            - (inv * inv * inv * cross) * x
        ).astype(jnp.bfloat16)

    row_loop(make_grad)
    ag_forward(1, 3)
    wgrad(1, trans_o, gpat)
    local["q"].wait()
    qc = go(copy(qboth.at[sq], qboth.at[sq], s_g.at[0], r_g.at[0], ydev))
    for k in range(ndp - 1, 0, -1):
        send_yo(dp + k, dp + k <= last)
        send_yo(dp - k, dp - k >= 0)
    send_yo(dp)
    local["ow"].wait()
    ag_wait_y(1)

    def attn(here, i):
        full = wall[1].reshape(up.shape[1], width)
        p = lax.dot_general(
            gpat[here, :], full, (((1,), (1,)), ((), ())), preferred_element_type=jnp.float32
        )
        for j in range(nt):
            pas[j, here, :] = p[:, j * HD : (j + 1) * HD]

    row_loop(attn)
    pa_copies = []
    for k in range(1, nt):
        gsend[k - 1] = pas[lax.rem(tn + k, nt)].astype(jnp.bfloat16)
        pa_copies.append(
            go(copy(gsend.at[k - 1], par.at[k - 1], s_pa.at[k - 1], r_pa.at[k - 1], tdev(k)))
        )

    acc[...] = two(dp)
    line_end(pl.ds(0, 2), *line_v)
    ysv[...] = acc[1 - sq].astype(jnp.bfloat16)
    yv = go(copy(ysv, yrv, s_yv.at[0], r_yv.at[0], ydev))

    total = pas[tn]
    for k, c in enumerate(pa_copies):
        c.wait_recv()
        total = total + par[k].astype(jnp.float32)
    gboth[sq] = total.astype(jnp.bfloat16)
    gc = go(copy(gboth.at[sq], gboth.at[sq], s_g.at[1], r_g.at[1], ydev))

    line(3, one, *line_o)
    line(2, one, *line_o)
    yv.wait_recv()
    acc[0] = acc[sq] + yrv[...].astype(jnp.float32)
    out_v = pltpu.make_async_copy(acc.at[0], wgv, s_out.at[0])
    out_v.start()
    line(1, one, *line_o)
    acc[1] = one(dp)
    line_end(1, *line_o)
    out_o = pltpu.make_async_copy(acc.at[1], wgo, s_out.at[1])
    out_o.start()
    qc.wait_recv()
    gc.wait_recv()
    out_q = pltpu.make_async_copy(qboth, q_out, s_out.at[2])
    out_q.start()
    out_g = pltpu.make_async_copy(gboth, g_out, s_out.at[3])
    out_g.start()
    for c, cond in sent:
        if cond is None:
            c.wait_send()
        else:
            pl.when(cond)(c.wait_send)
    for c in (out_v, out_o, out_q, out_g):
        c.wait()


def grad_call(ndp, nt, nbytes, states, resid, up, gain, vw, ow, ctx, q, starts):
    patches, width = states.shape
    rows = vw.shape[0]
    nblk = 2 * ndp
    nk = up.shape[1]
    bf, f32, i32 = jnp.bfloat16, jnp.float32, jnp.int32
    nrow = patches // 128
    total = starts.shape[1]
    vmem = pl.BlockSpec(memory_space=pltpu.VMEM)
    hbm = pl.BlockSpec(memory_space=pl.ANY)
    dma = pltpu.SemaphoreType.DMA
    return pl.pallas_call(
        functools.partial(grad_kernel, ndp, nt, nbytes),
        out_shape=(
            jax.ShapeDtypeStruct((rows, width), f32),
            jax.ShapeDtypeStruct((rows, width), f32),
            jax.ShapeDtypeStruct((2, patches, HD), bf),
            jax.ShapeDtypeStruct((2, patches, HD), bf),
            jax.ShapeDtypeStruct((2, 128), i32),
            jax.ShapeDtypeStruct((2, total + WIN), i32),
        ),
        in_specs=[hbm, hbm, hbm, vmem, hbm, hbm, hbm, hbm, vmem],
        out_specs=[hbm] * 4 + [vmem] * 2,
        scratch_shapes=[
            pltpu.VMEM((patches, width), bf),
            pltpu.VMEM((patches, width), bf),
            pltpu.VMEM((patches, nk), bf),
            pltpu.VMEM((patches, nk), bf),
            pltpu.VMEM((8, width), f32),
            pltpu.VMEM((2, nblk, rows, width), bf),
            pltpu.VMEM((2, nrow, 8, 128), f32),
            pltpu.VMEM((2, nt - 1, nrow, 8, 128), f32),
            pltpu.VMEM((2, nblk, rows, width), f32),
            pltpu.VMEM((2, rows, width), f32),
            pltpu.VMEM((ndp, 2, rows, width), bf),
            pltpu.VMEM((ndp, 2, rows, width), bf),
            pltpu.VMEM((rows, width), bf),
            pltpu.VMEM((rows, width), bf),
            pltpu.VMEM((ndp, rows, width), bf),
            pltpu.VMEM((ndp, rows, width), bf),
            pltpu.VMEM((ndp, rows, width), bf),
            pltpu.VMEM((ndp, rows, width), bf),
            pltpu.VMEM((nt, patches, HD), f32),
            pltpu.VMEM((nt - 1, patches, HD), bf),
            pltpu.VMEM((patches, width), f32),
            pltpu.VMEM((patches, width), bf),
            pltpu.VMEM((patches, width), bf),
            pltpu.VMEM((nk, patches), bf),
            pltpu.VMEM((nk, patches), bf),
            pltpu.VMEM((nt - 1, patches, HD), bf),
            pltpu.VMEM((2, patches, HD), bf),
            pltpu.VMEM((2, patches, HD), bf),
            dma((7,)), dma((2,)), dma((4,)),
            dma((2, 6 * ndp)), dma((2, nblk)),
            dma((2, nt - 1)), dma((2, nt - 1)),
            dma((ndp,)), dma((ndp,)), dma((ndp,)), dma((ndp,)),
            dma((ndp,)), dma((ndp,)), dma((ndp,)), dma((ndp,)),
            dma((ndp,)), dma((ndp,)), dma((1,)), dma((1,)),
            dma((nt - 1,)), dma((nt - 1,)), dma((2,)), dma((2,)),
        ],
        compiler_params=pltpu.CompilerParams(
            collective_id=0, has_side_effects=True, vmem_limit_bytes=60 * 1024 * 1024
        ),
    )(states, resid, up, gain, vw, ow, ctx, q, starts)


GROUP = 4


def byte_kernel(
    tab, bounds, g, q, wgv_in, wgo_in, keys_in, values_in, gk_out, gv_out, wgv, wgo,
    keys, values, gk, gv, expo, pgrad, bd, sums, table, s_k, s_v, o_k, o_v, s_w,
):
    total = g.shape[0]
    nwin = total // WIN
    nbytes = keys.shape[0]
    chunk = GROUP * BLK
    nchunk = nbytes // chunk
    lag = 1 + -(-(nwin - 1) // GROUP)
    ngroup = expo.shape[0] // GROUP
    scale = 1.0 / math.sqrt(HD)

    def rows_of(c):
        return pl.ds(pl.multiple_of(c * chunk, chunk), chunk)

    def load(c):
        here = rows_of(c)
        return (
            pltpu.make_async_copy(keys_in.at[here], keys.at[here], s_k.at[c]),
            pltpu.make_async_copy(values_in.at[here], values.at[here], s_v.at[c]),
        )

    def store(c):
        here = rows_of(c)
        return (
            pltpu.make_async_copy(gk.at[here], gk_out.at[here], o_k.at[c]),
            pltpu.make_async_copy(gv.at[here], gv_out.at[here], o_v.at[c]),
        )

    for c in range(nchunk):
        for x in load(c):
            x.start()
    passed = (
        pltpu.make_async_copy(wgv_in, wgv, s_w.at[0]),
        pltpu.make_async_copy(wgo_in, wgo, s_w.at[1]),
    )
    for x in passed:
        x.start()

    zero = jnp.zeros((WIN, HD), jnp.bfloat16)
    for w in range(nwin):
        bd[w, :WIN, :HD] = q[w * WIN : (w + 1) * WIN, :]
        bd[w, WIN:, HD:] = g[w * WIN : (w + 1) * WIN, :]
        bd[w, :WIN, HD:] = zero
        bd[w, WIN:, :HD] = zero
    bd[nwin] = jnp.zeros((2 * WIN, 2 * HD), jnp.bfloat16)
    sums[...] = jnp.zeros_like(sums)
    row = lax.broadcasted_iota(jnp.int32, (BLK, WIN), 0)

    def place(n):
        b, w = tab[0, n], tab[1, n]
        return (
            b, w, pl.ds(pl.multiple_of(b * BLK, BLK), BLK), pl.ds(pl.multiple_of(w * WIN, WIN), WIN)
        )

    def measure(group, _):
        @pl.when(group < nchunk)
        def _():
            for x in load(group):
                x.wait()

        for k in range(GROUP):
            n = group * GROUP + k
            b, w, here, lanes = place(n)
            both = jnp.concatenate([keys[here, :], values[here, :]], axis=1)
            s = lax.dot_general(
                both, bd[w], (((1,), (1,)), ((), ())), preferred_element_type=jnp.float32
            )
            lo = bounds[0:1, lanes] - b * BLK
            hi = bounds[1:2, lanes] - b * BLK
            e = jnp.where((row >= lo) & (row < hi), jnp.exp(s[:, :WIN] * scale), 0.0)
            pg = s[:, WIN:]
            expo[n] = e
            pgrad[n] = pg
            sums[0:1, lanes] += jnp.sum(e, axis=0, keepdims=True)
            sums[1:2, lanes] += jnp.sum(e * pg, axis=0, keepdims=True)
        return 0

    lax.fori_loop(0, ngroup, measure, 0)
    t = sums[0:1, :]
    inv = jnp.where(t > 0.0, 1.0 / jnp.where(t > 0.0, t, 1.0), 0.0)
    table[0:1, :] = inv
    table[1:2, :] = sums[1:2, :] * inv

    def apply(group, _):
        for k in range(GROUP):
            n = group * GROUP + k
            b, w, here, lanes = place(n)
            fresh = (n == 0) | (tab[0, jnp.maximum(n - 1, 0)] != b)
            p = expo[n] * table[0:1, lanes]
            sg = p * (pgrad[n] - table[1:2, lanes]) * scale
            both = jnp.concatenate([sg.astype(jnp.bfloat16), p.astype(jnp.bfloat16)], axis=1)
            out = jnp.dot(both, bd[w], preferred_element_type=jnp.float32).astype(jnp.bfloat16)

            @pl.when(fresh)
            def _():
                gk[here, :] = out[:, :HD]
                gv[here, :] = out[:, HD:]

            @pl.when(jnp.logical_not(fresh))
            def _():
                gk[here, :] += out[:, :HD]
                gv[here, :] += out[:, HD:]

        @pl.when((group >= lag) & (group - lag < nchunk))
        def _():
            for x in store(group - lag):
                x.start()

        return 0

    lax.fori_loop(0, ngroup, apply, 0)
    for c in range(max(ngroup - lag, 0), nchunk):
        for x in store(c):
            x.start()
    for c in range(nchunk):
        for x in store(c):
            x.wait()
    for x in passed:
        x.wait()


def byte_call(tab, bounds, g, q, wgv, wgo, keys, values):
    bf, f32 = jnp.bfloat16, jnp.float32
    nbytes = keys.shape[0]
    total = g.shape[0]
    nwin = total // WIN
    npair = -(-(nbytes // BLK + nwin - 1) // GROUP) * GROUP
    nchunk = nbytes // (GROUP * BLK)
    vmem = pl.BlockSpec(memory_space=pltpu.VMEM)
    hbm = pl.BlockSpec(memory_space=pl.ANY)
    dma = pltpu.SemaphoreType.DMA
    return pl.pallas_call(
        byte_kernel,
        out_shape=(
            jax.ShapeDtypeStruct(keys.shape, bf),
            jax.ShapeDtypeStruct(keys.shape, bf),
            jax.ShapeDtypeStruct(wgv.shape, f32),
            jax.ShapeDtypeStruct(wgo.shape, f32),
        ),
        in_specs=[pl.BlockSpec(memory_space=pltpu.SMEM), vmem, vmem, vmem] + [hbm] * 4,
        out_specs=[hbm] * 4,
        scratch_shapes=[
            pltpu.VMEM(keys.shape, bf), pltpu.VMEM(keys.shape, bf),
            pltpu.VMEM(keys.shape, bf), pltpu.VMEM(keys.shape, bf),
            pltpu.VMEM((npair, BLK, WIN), f32), pltpu.VMEM((npair, BLK, WIN), f32),
            pltpu.VMEM((nwin + 1, 2 * WIN, 2 * HD), bf),
            pltpu.VMEM((8, total + WIN), f32), pltpu.VMEM((8, total + WIN), f32),
            dma((nchunk,)), dma((nchunk,)), dma((nchunk,)), dma((nchunk,)), dma((2,)),
        ],
        compiler_params=pltpu.CompilerParams(vmem_limit_bytes=60 * 1024 * 1024),
    )(tab, bounds, g, q, wgv, wgo, keys, values)


def on_device_kernels(
    ndp, nt, patch_states, residual_grad, upstream_value, norm_gain, value_weight, out_weight,
    attn_out, queries, byte_keys, byte_values, patch_starts,
):
    nbytes = byte_keys.shape[1]
    wgv, wgo, g, q, tab, bounds = grad_call(
        ndp, nt, nbytes, patch_states[0], residual_grad[0], upstream_value[0],
        norm_gain.reshape(-1, 128), value_weight, out_weight, attn_out[0], queries[0], patch_starts,
    )
    gk, gv, wgv, wgo = byte_call(
        tab, bounds, g.reshape(-1, HD), q.reshape(-1, HD), wgv, wgo, byte_keys[0], byte_values[0]
    )
    return (wgv, wgo, gk[None], gv[None])


def solution(mesh):
    ndp, nseq, nt = mesh.shape["dp"], mesh.shape["seq"], mesh.shape["tensor"]
    use_kernels = nseq == 2 and ndp == 4
    body = functools.partial(on_device_kernels, ndp, nt) if use_kernels else on_device
    return jax.shard_map(
        body,
        mesh=mesh,
        in_specs=(
            P("dp", "seq", "tensor"),
            P("dp", "seq", "tensor"),
            P("dp", "seq", None),
            P("tensor"),
            P(("dp", "seq"), "tensor"),
            P(("dp", "seq"), "tensor"),
            P("dp", "seq", None),
            P("dp", "seq", "tensor"),
            P("dp", "seq", "tensor"),
            P("dp", "seq", "tensor"),
            P("dp", None),
        ),
        out_specs=(
            P(("dp", "seq"), "tensor"),
            P(("dp", "seq"), "tensor"),
            P("dp", "seq", "tensor"),
            P("dp", "seq", "tensor"),
        ),
        check_vma=False,
    )
```

```python
import functools
import math

import jax
import jax.numpy as jnp
from jax import lax
from jax.experimental import pallas as pl
from jax.experimental.pallas import tpu as pltpu
from jax.sharding import PartitionSpec as P

HD = 128


def member_sum(member32, terms):
    return lax.dot_general(
        member32,
        terms,
        (((0,), (0,)), ((), ())),
        precision=lax.Precision.HIGHEST,
        preferred_element_type=jnp.float32,
    )


def member_spread(member32, totals):
    return jnp.dot(
        member32, totals, precision=lax.Precision.HIGHEST, preferred_element_type=jnp.float32
    )


def cross_backward(member, segment_rows, keys, values, head_width):
    nbytes = keys.shape[0]
    heads = keys.shape[1] // HD
    scale = 1.0 / math.sqrt(HD)
    member32 = member.astype(jnp.float32)
    picked = jnp.dot(member, segment_rows, preferred_element_type=jnp.float32).astype(jnp.bfloat16)
    grad_f = picked[:, :head_width].astype(jnp.float32).reshape(nbytes, heads, HD)
    query_f = picked[:, head_width:].astype(jnp.float32).reshape(nbytes, heads, HD)
    keys_f = keys.astype(jnp.float32).reshape(nbytes, heads, HD)
    values_f = values.astype(jnp.float32).reshape(nbytes, heads, HD)
    scores = jnp.sum(query_f * keys_f, axis=-1) * scale
    expo = jnp.exp(scores)
    totals = member_spread(member32, member_sum(member32, expo))
    probs = expo / totals
    grad_values = (probs[..., None] * grad_f).reshape(nbytes, heads * HD).astype(jnp.bfloat16)
    prob_grad = jnp.sum(grad_f * values_f, axis=-1)
    mass = member_spread(member32, member_sum(member32, probs * prob_grad))
    score_grad = probs * (prob_grad - mass)
    grad_keys = (
        (score_grad[..., None] * query_f * scale).reshape(nbytes, heads * HD).astype(jnp.bfloat16)
    )
    return (grad_keys, grad_values)


def contract_rows(left, right):
    return lax.dot_general(
        left, right, (((0,), (0,)), ((), ())), preferred_element_type=jnp.float32
    )


def on_device(
    patch_states,
    residual_grad,
    upstream_value,
    norm_gain,
    value_weight,
    out_weight,
    attn_out,
    queries,
    byte_keys,
    byte_values,
    patch_starts,
):
    states = patch_states[0]
    patches = states.shape[0]
    width_local = states.shape[1]
    model_width = width_local * lax.axis_size("tensor")
    states32 = states.astype(jnp.float32)
    gain32 = norm_gain.astype(jnp.float32)
    upstream = upstream_value[0]
    context = attn_out[0]
    value_full, out_full = (
        lax.all_gather(value_weight, ("dp", "seq"), axis=0, tiled=True),
        lax.all_gather(out_weight, ("dp", "seq"), axis=0, tiled=True),
    )
    grad_normed = jnp.dot(upstream, value_full, preferred_element_type=jnp.float32)
    square_part = jnp.sum(states32 * states32, axis=1)
    cross_part = jnp.sum(grad_normed * gain32 * states32, axis=1)
    square_sum, cross_sum = lax.psum((square_part, cross_part), "tensor")
    inv_rms = lax.rsqrt(square_sum / model_width + 1e-05)
    normed = (states32 * inv_rms[:, None] * gain32).astype(jnp.bfloat16)
    grad_patch = (
        residual_grad[0].astype(jnp.float32)
        + inv_rms[:, None] * gain32 * grad_normed
        - (inv_rms**3)[:, None] * states32 * (cross_sum / model_width)[:, None]
    ).astype(jnp.bfloat16)
    partial_attn = lax.dot_general(
        grad_patch, out_full, (((1,), (1,)), ((), ())), preferred_element_type=jnp.float32
    )
    columns = upstream
    wgrad_value = lax.psum_scatter(
        contract_rows(columns, normed), ("dp", "seq"), scatter_dimension=0, tiled=True
    )
    columns = context
    wgrad_out = lax.psum_scatter(
        contract_rows(columns, grad_patch), ("dp", "seq"), scatter_dimension=0, tiled=True
    )
    attn_all = lax.psum(partial_attn, "tensor").astype(jnp.bfloat16)
    head_width = queries.shape[2]
    grad_attn = lax.dynamic_slice_in_dim(
        attn_all, lax.axis_index("tensor") * head_width, head_width, 1
    )
    starts = patch_starts[0]
    total_patches = starts.shape[0]
    seq_count = lax.axis_size("seq")
    seq_pos = lax.axis_index("seq")
    byte_count = byte_keys.shape[1]
    window_len = 2 * patches
    owners = starts // byte_count
    shard_ids = jnp.arange(seq_count, dtype=jnp.int32)
    firsts = jnp.sum((owners[None, :] < shard_ids[:, None]).astype(jnp.int32), axis=1)
    my_first = jnp.sum(firsts * (shard_ids == seq_pos).astype(jnp.int32))
    payload = jnp.concatenate([grad_attn, queries[0]], axis=1)
    padded_starts = jnp.concatenate(
        [starts, jnp.full((window_len,), 2 * total_patches * byte_count + byte_count, jnp.int32)]
    )
    local_starts = lax.dynamic_slice_in_dim(padded_starts, my_first, window_len)
    positions = seq_pos * byte_count + jnp.arange(byte_count, dtype=jnp.int32)
    reached = local_starts[None, :] <= positions[:, None]
    after = jnp.concatenate([reached[:, 1:], jnp.zeros((byte_count, 1), bool)], axis=1)
    member = (reached & jnp.logical_not(after)).astype(jnp.bfloat16)
    mine = seq_pos * patches + jnp.arange(patches, dtype=jnp.int32)
    targets = lax.dynamic_slice_in_dim(owners, seq_pos * patches, patches)
    target_first = jnp.sum((owners[None, :] < targets[:, None]).astype(jnp.int32), axis=1)
    slots = mine - jnp.maximum(seq_pos * patches, target_first)
    dest = targets * patches + slots
    place = (jnp.arange(seq_count * patches, dtype=jnp.int32)[:, None] == dest[None, :]).astype(
        jnp.bfloat16
    )
    outgoing = jnp.dot(place, payload, preferred_element_type=jnp.float32).astype(jnp.bfloat16)
    outgoing = outgoing.reshape(seq_count, patches, 2 * head_width)
    incoming = lax.all_to_all(outgoing, "seq", split_axis=0, concat_axis=0, tiled=True)
    wanted = my_first + jnp.arange(window_len, dtype=jnp.int32)
    sources = wanted // patches
    received_row = sources * patches + wanted - jnp.maximum(sources * patches, my_first)
    select = (
        received_row[:, None] == jnp.arange(seq_count * patches, dtype=jnp.int32)[None, :]
    ).astype(jnp.bfloat16)
    segment_rows = jnp.dot(
        select,
        incoming.reshape(seq_count * patches, 2 * head_width),
        preferred_element_type=jnp.float32,
    ).astype(jnp.bfloat16)
    grad_keys, grad_values = cross_backward(
        member, segment_rows, byte_keys[0], byte_values[0], head_width
    )
    return (wgrad_value, wgrad_out, grad_keys[None], grad_values[None])


BLK = 256
WIN = 128


def grad_kernel(
    ndp, nt, nbytes, states_in, resid_in, up_in, gain_in, vw, ow, ctx_in, q_in, starts,
    wgv, wgo, g_out, q_out, tab, bounds,
    states, resid, up, ctx, gain, wall, sqs, sqr, part, acc, acco, accz, rbz, lbz, ysz, yrz, rbv, lbv, ysv, yrv, rbo, lbo, yso, yro,
    pas, par, gn, nrm, gpat, trans_v, trans_o, gsend, gboth, qboth,
    s_in, s_own, s_out, s_ag, r_ag, s_sq, r_sq, s_rv, r_rv, s_lv, r_lv, s_ro, r_ro, s_lo, r_lo,
    s_rz, r_rz, s_lz, r_lz, s_yo, r_yo, s_yv, r_yv, s_pa, r_pa, s_g, r_g,
):
    dp, sq, tn = lax.axis_index("dp"), lax.axis_index("seq"), lax.axis_index("tensor")
    patches, width = states.shape
    model = width * nt
    last = ndp - 1
    mine = dp * 2 + sq
    tall = 128
    nrow = patches // tall
    ncol = width // 256

    right, left = (dp + 1, sq, tn), (dp - 1, sq, tn)
    ydev = (dp, 1 - sq, tn)

    def tdev(k):
        return (dp, sq, lax.rem(tn + k, nt))

    def copy(src, dst, ssem, rsem, dev):
        return pltpu.make_async_remote_copy(
            src_ref=src, dst_ref=dst, send_sem=ssem, recv_sem=rsem,
            device_id=dev, device_id_type=pl.DeviceIdType.MESH,
        )

    local = {}
    for i, (name, src, dst) in enumerate(
        (("states", states_in, states), ("up", up_in, up), ("resid", resid_in, resid),
         ("ctx", ctx_in, ctx), ("q", q_in, qboth.at[sq]), ("vw", vw, wall.at[0, mine]),
         ("ow", ow, wall.at[1, mine]))
    ):
        local[name] = pltpu.make_async_copy(src, dst, s_in.at[i])
        local[name].start()

    barrier = pltpu.get_barrier_semaphore()
    peers = [(lax.rem(dp + k, ndp), sq, tn) for k in range(1, ndp)]
    peers += [tdev(k) for k in range(1, nt)] + [ydev]
    for dev in peers:
        pl.semaphore_signal(barrier, inc=1, device_id=dev, device_id_type=pl.DeviceIdType.MESH)
    pl.semaphore_wait(barrier, len(peers))

    sent = []

    def go(c, cond=None):
        if cond is None:
            c.start()
        else:
            pl.when(cond)(c.start)
        sent.append((c, cond))
        return c

    weights = (vw, ow)

    def half(h):
        return pl.ds(h * (vw.shape[0] // 2), vw.shape[0] // 2)

    def shard(w, zz, yy, h, dev, k, own=False):
        slot = zz * 2 + yy
        block = wall.at[w, slot, half(h)]
        src = weights[w].at[half(h)] if own else block
        return copy(src, block, s_ag.at[w, h, k], r_ag.at[w, h, slot], dev)

    def ag_own_z(w, h, ends=True, inner=True):
        for dev, onward, edge, k in ((right, dp < last, dp == 0, 0), (left, dp > 0, dp == last, 1)):
            if ends:
                go(shard(w, dp, sq, h, dev, k, True), edge)
            if inner:
                go(shard(w, dp, sq, h, dev, k, True), onward & jnp.logical_not(edge))

    def ag_own_y(w, h):
        go(shard(w, dp, sq, h, ydev, 2, True))

    def ag_forward(w, s, h):
        for zz, here, dev, onward, k in (
            (dp - s, dp - s >= 0, right, dp < last, 3 * s),
            (dp + s, dp + s <= last, left, dp > 0, 3 * ndp + 3 * s),
        ):
            pl.when(here)(shard(w, zz, sq, h, dev, k).wait_recv)
            go(shard(w, zz, sq, h, dev, k), here & onward)
            spread = here if w == 0 or s > 1 else here & ((zz == 0) | (zz == last))
            go(shard(w, zz, sq, h, ydev, k + 1), spread)

    def ag_cross(w, h):
        inner = (dp > 0) & (dp < last)
        pl.when(inner)(shard(w, dp, 1 - sq, h, ydev, 2).wait_recv)
        go(shard(w, dp, 1 - sq, h, right, 11), inner)
        go(shard(w, dp, 1 - sq, h, left, 12), inner)

    def ag_wait_y(w):
        for zz in range(ndp):
            for h in range(2):
                wait = shard(w, zz, 1 - sq, h, ydev, 2).wait_recv
                if w == 0 or zz in (0, last):
                    wait()
                else:
                    pl.when(dp != zz)(wait)

    def row_loop(fn):
        def body(i, _):
            fn(pl.ds(pl.multiple_of(i * tall, tall), tall), i)
            return 0

        lax.fori_loop(0, nrow, body, 0)

    def to_row(col):
        return jnp.broadcast_to(col, (tall, 128)).T[:8]

    def share(which):
        return [
            go(copy(sqs.at[which], sqr.at[which, k - 1], s_sq.at[which, k - 1],
                    r_sq.at[which, k - 1], tdev(k)))
            for k in range(1, nt)
        ]

    def total_col(which, i):
        rows = sqs[which, i]
        for k in range(nt - 1):
            rows = rows + sqr[which, k, i]
        return jnp.broadcast_to(rows[0:1, :], (128, tall)).T[:, 0:1]

    def inverse(i):
        return lax.rsqrt(total_col(0, i) / model + 1e-05)

    def square(here, i):
        x = states[here, :].astype(jnp.float32)
        sqs[0, i] = to_row(jnp.sum(x * x, axis=1, keepdims=True))

    def normalise(here, i):
        x = states[here, :].astype(jnp.float32)
        nrm[here, :] = (x * inverse(i) * gain[0:1, :]).astype(jnp.bfloat16)

    def wgrad(w, trans, factor):
        nblk, rows_per = part.shape[1], part.shape[2]

        def body(c, _):
            cols = pl.ds(pl.multiple_of(c * 256, 256), 256)
            out = jnp.dot(trans[...], factor[:, cols], preferred_element_type=jnp.float32)
            part[w, :, :, cols] = out.reshape(nblk, rows_per, 256)
            return 0

        lax.fori_loop(0, ncol, body, 0)

    def part_v(zz, h):
        return part[0, zz * 2 + h]

    def part_z(zz, h):
        return part[1, zz * 2 + h, half(1)]

    def part_o(zz, h):
        yo(zz, h).wait_recv()
        return part[1, zz * 2 + sq, half(h)] + yro[zz, h].astype(jnp.float32)

    def hops(d, h, buf_r, buf_l, s_r, r_r, s_l, r_l):
        for zz, valid, dev, fed, buf, ss, rs in (
            (dp + d, dp + d <= last, right, dp > 0, buf_r, s_r, r_r),
            (dp - d, dp - d >= 0, left, dp < last, buf_l, s_l, r_l),
        ):
            c = copy(buf.at[zz, h], buf.at[zz, h], ss.at[d - 1, h], rs.at[zz, h], dev)
            yield zz, valid, fed, buf, c

    def line_open(get, bufs, halves=(0, 1)):
        for d in range(last, 0, -1):
            for h in halves:
                for zz, valid, fed, buf, c in hops(d, h, *bufs):
                    opening = valid & jnp.logical_not(fed)

                    @pl.when(opening)
                    def _(zz=zz, h=h, buf=buf):
                        buf[zz, h] = get(zz, h).astype(jnp.bfloat16)

                    go(c, opening)

    def line(d, h, get, bufs):
        for zz, valid, fed, buf, c in hops(d, h, *bufs):

            @pl.when(valid & fed)
            def _(zz=zz, buf=buf, c=c):
                mine_part = get(zz, h)
                c.wait_recv()
                buf[zz, h] = (mine_part + buf[zz, h].astype(jnp.float32)).astype(jnp.bfloat16)

            go(c, valid & fed)

    def line_end(h, acc, bufs):
        buf_r, buf_l, s_r, r_r, s_l, r_l = bufs
        for fed, dev, buf, ss, rs in (
            (dp > 0, right, buf_r, s_r, r_r),
            (dp < last, left, buf_l, s_l, r_l),
        ):
            c = copy(buf.at[dp, h], buf.at[dp, h], ss.at[0, h], rs.at[dp, h], dev)

            @pl.when(fed)
            def _(c=c, buf=buf):
                c.wait_recv()
                acc[h] += buf[dp, h].astype(jnp.float32)

    line_v = (rbv, lbv, s_rv, r_rv, s_lv, r_lv)
    line_o = (rbo, lbo, s_ro, r_ro, s_lo, r_lo)
    line_z = (rbz, lbz, s_rz, r_rz, s_lz, r_lz)

    def yo(zz, h):
        return copy(yso.at[zz, h], yro.at[zz, h], s_yo.at[zz, h], r_yo.at[zz, h], ydev)

    def send_yo(zz, h, cond=None):
        def fill():
            yso[zz, h] = part[1, zz * 2 + (1 - sq), half(h)].astype(jnp.bfloat16)

        fill() if cond is None else pl.when(cond)(fill)
        go(yo(zz, h), cond)

    for h in range(2):
        ag_own_z(0, h)
        ag_own_y(0, h)
    for i in range(width // 128):
        gain[:, i * 128 : (i + 1) * 128] = jnp.broadcast_to(
            gain_in[i : i + 1, :].astype(jnp.float32), (8, 128)
        )
    local["states"].wait()
    row_loop(square)
    sq_copies = share(0)
    local["up"].wait()
    trans_v[...] = up[...].T

    first = starts[0:1, :] - sq * nbytes
    row8 = jnp.broadcast_to(first, (8, first.shape[1]))
    lane = lax.broadcasted_iota(jnp.int32, row8.shape, 1)
    after = jnp.where(
        lane == first.shape[1] - 1, 2 * nbytes, pltpu.roll(row8, first.shape[1] - 1, 1)
    )
    far = jnp.full((1, WIN), 4 * nbytes, jnp.int32)
    bounds[0:1, : first.shape[1]] = first
    bounds[1:2, : first.shape[1]] = after[0:1, :]
    bounds[0:1, first.shape[1] :] = far
    bounds[1:2, first.shape[1] :] = far

    ag_forward(0, 1, 0)
    for c in sq_copies:
        c.wait_recv()
    row_loop(normalise)
    ag_forward(0, 1, 1)
    wgrad(0, trans_v, nrm)
    for h in range(2):
        ag_own_z(1, h, inner=False)
    line_open(part_v, line_v)
    ag_forward(0, 2, 0)
    nblocks = nbytes // BLK
    ends = lax.broadcasted_iota(jnp.int32, (nblocks, first.shape[1]), 0) * BLK + (BLK - 1)
    reach = (jnp.broadcast_to(first, ends.shape) <= ends).astype(jnp.int32)
    high = (jnp.sum(reach, axis=1, keepdims=True) - 1) // WIN
    low = (jnp.sum((first <= 0).astype(jnp.int32), axis=1, keepdims=True) - 1) // WIN
    step = lax.broadcasted_iota(jnp.int32, (nblocks, 128), 0) + high - low
    pair = lax.broadcasted_iota(jnp.int32, (nblocks, 128), 1)
    block_of = jnp.sum((step < pair).astype(jnp.int32), axis=0, keepdims=True)
    window = lax.broadcasted_iota(jnp.int32, (1, 128), 1) - block_of + low
    done = block_of >= nblocks
    tab[0:1, :] = jnp.where(done, nblocks - 1, block_of)
    tab[1:2, :] = jnp.where(done, first.shape[1] // WIN, window)

    ag_forward(0, 2, 1)
    local["ctx"].wait()
    trans_o[...] = ctx[...].T
    for h in range(2):
        ag_forward(0, 3, h)
        ag_own_z(1, h, ends=False)
        ag_own_y(1, h)
    ag_forward(1, 1, 0)
    local["vw"].wait()
    ag_wait_y(0)
    ag_forward(1, 1, 1)

    def project(here, i):
        full = wall[0].reshape(up.shape[1], width)
        g = jnp.dot(up[here, :], full, preferred_element_type=jnp.float32)
        gn[here, :] = g
        x = states[here, :].astype(jnp.float32)
        sqs[1, i] = to_row(jnp.sum(g * gain[0:1, :] * x, axis=1, keepdims=True))

    row_loop(project)
    cr_copies = share(1)
    ag_cross(1, 0)
    ag_forward(1, 2, 0)
    ag_cross(1, 1)
    line(2, 0, part_v, line_v)
    ag_forward(1, 2, 1)
    line(2, 1, part_v, line_v)
    local["resid"].wait()
    for c in cr_copies:
        c.wait_recv()

    def make_grad(here, i):
        inv = inverse(i)
        cross = total_col(1, i) / model
        x = states[here, :].astype(jnp.float32)
        gpat[here, :] = (
            resid[here, :].astype(jnp.float32)
            + inv * gain[0:1, :] * gn[here, :]
            - (inv * inv * inv * cross) * x
        ).astype(jnp.bfloat16)

    row_loop(make_grad)
    ag_forward(1, 3, 0)
    ag_forward(1, 3, 1)
    local["q"].wait()
    qc = go(copy(qboth.at[sq], qboth.at[sq], s_g.at[0], r_g.at[0], ydev))
    wgrad(1, trans_o, gpat)
    line_open(part_z, line_z)
    for k in range(ndp - 1, 0, -1):
        send_yo(dp + k, 0, dp + k <= last)
        send_yo(dp - k, 0, dp - k >= 0)
    send_yo(dp, 0)
    for h in range(2):
        line(1, h, part_v, line_v)
    for h in range(2):
        line(2, h, part_z, line_z)
    local["ow"].wait()
    ag_wait_y(1)

    def tile(i):
        return pl.ds(i * tall, tall)

    def pa(i, k):
        return copy(gsend.at[k - 1, tile(i)], par.at[k - 1, tile(i)], s_pa.at[k - 1, i],
                    r_pa.at[k - 1, i], tdev(k))

    for i in range(nrow):
        full = wall[1].reshape(up.shape[1], width)
        p = lax.dot_general(
            gpat[tile(i), :], full, (((1,), (1,)), ((), ())), preferred_element_type=jnp.float32
        )
        for j in range(nt):
            pas[j, tile(i), :] = p[:, j * HD : (j + 1) * HD]
        for k in range(1, nt):
            gsend[k - 1, tile(i)] = pas[lax.rem(tn + k, nt), tile(i)].astype(jnp.bfloat16)
            go(pa(i, k))

    for h in range(2):
        acc[h] = part_v(dp, h)
        line_end(h, acc, line_v)
    ysv[...] = acc[1 - sq].astype(jnp.bfloat16)
    yv = go(copy(ysv, yrv, s_yv.at[0], r_yv.at[0], ydev))
    line_open(part_o, line_o, (0,))
    for h in range(2):
        line(1, h, part_z, line_z)
    line(2, 0, part_o, line_o)
    gc = []
    for i in range(nrow):
        total = pas[tn, tile(i)]
        for k in range(1, nt):
            pa(i, k).wait_recv()
            total = total + par[k - 1, tile(i)].astype(jnp.float32)
        gboth[sq, tile(i)] = total.astype(jnp.bfloat16)
        block = gboth.at[sq, tile(i)]
        gc.append(go(copy(block, block, s_g.at[1 + i], r_g.at[1 + i], ydev)))
    for h in range(2):
        accz[h] = part_z(dp, h)
        line_end(h, accz, line_z)
    ysz[...] = accz[1 - sq].astype(jnp.bfloat16)
    yz = go(copy(ysz, yrz, s_yv.at[1], r_yv.at[1], ydev))
    line(1, 0, part_o, line_o)
    yv.wait_recv()
    acc[0] = acc[sq] + yrv[...].astype(jnp.float32)
    out_v = pltpu.make_async_copy(acc.at[0], wgv, s_out.at[0])
    out_v.start()
    acco[0] = part_o(dp, 0)
    line_end(0, acco, line_o)
    yz.wait_recv()
    acco[1] = accz[sq] + yrz[...].astype(jnp.float32)
    out_o = pltpu.make_async_copy(acco, wgo, s_out.at[1])
    out_o.start()
    qc.wait_recv()
    for c in gc:
        c.wait_recv()
    out_q = pltpu.make_async_copy(qboth, q_out, s_out.at[2])
    out_q.start()
    out_g = pltpu.make_async_copy(gboth, g_out, s_out.at[3])
    out_g.start()
    for c, cond in sent:
        if cond is None:
            c.wait_send()
        else:
            pl.when(cond)(c.wait_send)
    for c in (out_v, out_o, out_q, out_g):
        c.wait()


def grad_call(ndp, nt, nbytes, states, resid, up, gain, vw, ow, ctx, q, starts):
    patches, width = states.shape
    rows = vw.shape[0]
    nblk = 2 * ndp
    nk = up.shape[1]
    bf, f32, i32 = jnp.bfloat16, jnp.float32, jnp.int32
    nrow = patches // 128
    total = starts.shape[1]
    vmem = pl.BlockSpec(memory_space=pltpu.VMEM)
    hbm = pl.BlockSpec(memory_space=pl.ANY)
    dma = pltpu.SemaphoreType.DMA
    return pl.pallas_call(
        functools.partial(grad_kernel, ndp, nt, nbytes),
        out_shape=(
            jax.ShapeDtypeStruct((rows, width), f32),
            jax.ShapeDtypeStruct((2, rows // 2, width), f32),
            jax.ShapeDtypeStruct((2, patches, HD), bf),
            jax.ShapeDtypeStruct((2, patches, HD), bf),
            jax.ShapeDtypeStruct((2, 128), i32),
            jax.ShapeDtypeStruct((2, total + WIN), i32),
        ),
        in_specs=[hbm, hbm, hbm, vmem, hbm, hbm, hbm, hbm, vmem],
        out_specs=[hbm] * 4 + [vmem] * 2,
        scratch_shapes=[
            pltpu.VMEM((patches, width), bf),
            pltpu.VMEM((patches, width), bf),
            pltpu.VMEM((patches, nk), bf),
            pltpu.VMEM((patches, nk), bf),
            pltpu.VMEM((8, width), f32),
            pltpu.VMEM((2, nblk, rows, width), bf),
            pltpu.VMEM((2, nrow, 8, 128), f32),
            pltpu.VMEM((2, nt - 1, nrow, 8, 128), f32),
            pltpu.VMEM((2, nblk, rows, width), f32),
            pltpu.VMEM((2, rows, width), f32),
            pltpu.VMEM((2, rows // 2, width), f32),
            pltpu.VMEM((2, rows // 2, width), f32),
            pltpu.VMEM((ndp, 2, rows // 2, width), bf),
            pltpu.VMEM((ndp, 2, rows // 2, width), bf),
            pltpu.VMEM((rows // 2, width), bf),
            pltpu.VMEM((rows // 2, width), bf),
            pltpu.VMEM((ndp, 2, rows, width), bf),
            pltpu.VMEM((ndp, 2, rows, width), bf),
            pltpu.VMEM((rows, width), bf),
            pltpu.VMEM((rows, width), bf),
            pltpu.VMEM((ndp, 2, rows // 2, width), bf),
            pltpu.VMEM((ndp, 2, rows // 2, width), bf),
            pltpu.VMEM((ndp, 2, rows // 2, width), bf),
            pltpu.VMEM((ndp, 2, rows // 2, width), bf),
            pltpu.VMEM((nt, patches, HD), f32),
            pltpu.VMEM((nt - 1, patches, HD), bf),
            pltpu.VMEM((patches, width), f32),
            pltpu.VMEM((patches, width), bf),
            pltpu.VMEM((patches, width), bf),
            pltpu.VMEM((nk, patches), bf),
            pltpu.VMEM((nk, patches), bf),
            pltpu.VMEM((nt - 1, patches, HD), bf),
            pltpu.VMEM((2, patches, HD), bf),
            pltpu.VMEM((2, patches, HD), bf),
            dma((7,)), dma((2,)), dma((4,)),
            dma((2, 2, 6 * ndp)), dma((2, 2, nblk)),
            dma((2, nt - 1)), dma((2, nt - 1)),
            dma((ndp, 2)), dma((ndp, 2)), dma((ndp, 2)), dma((ndp, 2)),
            dma((ndp, 2)), dma((ndp, 2)), dma((ndp, 2)), dma((ndp, 2)),
            dma((ndp, 2)), dma((ndp, 2)), dma((ndp, 2)), dma((ndp, 2)),
            dma((ndp, 2)), dma((ndp, 2)), dma((2,)), dma((2,)),
            dma((nt - 1, nrow)), dma((nt - 1, nrow)), dma((1 + nrow,)), dma((1 + nrow,)),
        ],
        compiler_params=pltpu.CompilerParams(
            collective_id=0, has_side_effects=True, vmem_limit_bytes=60 * 1024 * 1024
        ),
    )(states, resid, up, gain, vw, ow, ctx, q, starts)


GROUP = 8


def byte_kernel(
    tab, bounds, g, q, wgv_in, wgo_in, keys_in, values_in, gk_out, gv_out, wgv, wgo,
    keys, values, gk, gv, expo, pgrad, bd, sums, table, held, s_k, s_v, o_k, o_v, s_w,
):
    total = g.shape[0]
    nwin = total // WIN
    nbytes = keys.shape[0]
    chunk = GROUP * BLK
    nchunk = nbytes // chunk
    lag = 1 + -(-(nwin - 1) // GROUP)
    ngroup = expo.shape[0] // GROUP
    scale = 1.0 / math.sqrt(HD)

    def rows_of(c):
        return pl.ds(pl.multiple_of(c * chunk, chunk), chunk)

    def load(c):
        here = rows_of(c)
        return (
            pltpu.make_async_copy(keys_in.at[here], keys.at[here], s_k.at[c]),
            pltpu.make_async_copy(values_in.at[here], values.at[here], s_v.at[c]),
        )

    def store(c):
        here = rows_of(c)
        return (
            pltpu.make_async_copy(gk.at[here], gk_out.at[here], o_k.at[c]),
            pltpu.make_async_copy(gv.at[here], gv_out.at[here], o_v.at[c]),
        )

    for c in range(nchunk):
        for x in load(c):
            x.start()
    carried = ((wgv_in, wgv), (wgo_in, wgo))
    taken = [pltpu.make_async_copy(a, held.at[i], s_w.at[i]) for i, (a, _) in enumerate(carried)]
    passed = [pltpu.make_async_copy(held.at[i], b, s_w.at[2 + i]) for i, (_, b) in enumerate(carried)]
    for x in taken:
        x.start()

    zero = jnp.zeros((WIN, HD), jnp.bfloat16)
    for w in range(nwin):
        bd[w, :WIN, :HD] = q[w * WIN : (w + 1) * WIN, :]
        bd[w, WIN:, HD:] = g[w * WIN : (w + 1) * WIN, :]
        bd[w, :WIN, HD:] = zero
        bd[w, WIN:, :HD] = zero
    bd[nwin] = jnp.zeros((2 * WIN, 2 * HD), jnp.bfloat16)
    sums[...] = jnp.zeros_like(sums)
    row = lax.broadcasted_iota(jnp.int32, (BLK, WIN), 0)

    def place(n):
        b, w = tab[0, n], tab[1, n]
        return (
            b, w, pl.ds(pl.multiple_of(b * BLK, BLK), BLK), pl.ds(pl.multiple_of(w * WIN, WIN), WIN)
        )

    def measure(group, _):
        @pl.when(group < nchunk)
        def _():
            for x in load(group):
                x.wait()

        for k in range(GROUP):
            n = group * GROUP + k
            b, w, here, lanes = place(n)
            both = jnp.concatenate([keys[here, :], values[here, :]], axis=1)
            s = lax.dot_general(
                both, bd[w], (((1,), (1,)), ((), ())), preferred_element_type=jnp.float32
            )
            lo = bounds[0:1, lanes] - b * BLK
            hi = bounds[1:2, lanes] - b * BLK
            e = jnp.where((row >= lo) & (row < hi), jnp.exp(s[:, :WIN] * scale), 0.0)
            pg = s[:, WIN:]
            expo[n] = e
            pgrad[n] = pg
            sums[0:1, lanes] += jnp.sum(e, axis=0, keepdims=True)
            sums[1:2, lanes] += jnp.sum(e * pg, axis=0, keepdims=True)
        return 0

    lax.fori_loop(0, ngroup, measure, 0)
    for x, y in zip(taken, passed):
        x.wait()
        y.start()
    t = sums[0:1, :]
    inv = jnp.where(t > 0.0, 1.0 / jnp.where(t > 0.0, t, 1.0), 0.0)
    table[0:1, :] = inv
    table[1:2, :] = sums[1:2, :] * inv

    def apply(group, _):
        first = group * GROUP
        prior = jnp.maximum(first - 1, 0)
        before = pl.ds(pl.multiple_of(tab[0, prior] * BLK, BLK), BLK)
        held_k, held_v = gk[before, :], gv[before, :]
        for k in range(GROUP):
            n = first + k
            b, w, here, lanes = place(n)
            same = tab[0, jnp.maximum(n - 1, 0)] == b
            same = same & (n > 0) if k == 0 else same
            p = expo[n] * table[0:1, lanes]
            sg = p * (pgrad[n] - table[1:2, lanes]) * scale
            both = jnp.concatenate([sg.astype(jnp.bfloat16), p.astype(jnp.bfloat16)], axis=1)
            out = jnp.dot(both, bd[w], preferred_element_type=jnp.float32).astype(jnp.bfloat16)
            held_k = out[:, :HD] + jnp.where(same, held_k, jnp.zeros_like(held_k))
            held_v = out[:, HD:] + jnp.where(same, held_v, jnp.zeros_like(held_v))
            gk[here, :] = held_k
            gv[here, :] = held_v

        @pl.when((group >= lag) & (group - lag < nchunk))
        def _():
            for x in store(group - lag):
                x.start()

        return 0

    lax.fori_loop(0, ngroup, apply, 0)
    for c in range(max(ngroup - lag, 0), nchunk):
        for x in store(c):
            x.start()
    for c in range(nchunk):
        for x in store(c):
            x.wait()
    for x in passed:
        x.wait()


def byte_call(tab, bounds, g, q, wgv, wgo, keys, values):
    bf, f32 = jnp.bfloat16, jnp.float32
    nbytes = keys.shape[0]
    total = g.shape[0]
    nwin = total // WIN
    npair = -(-(nbytes // BLK + nwin - 1) // GROUP) * GROUP
    nchunk = nbytes // (GROUP * BLK)
    vmem = pl.BlockSpec(memory_space=pltpu.VMEM)
    hbm = pl.BlockSpec(memory_space=pl.ANY)
    dma = pltpu.SemaphoreType.DMA
    return pl.pallas_call(
        byte_kernel,
        out_shape=(
            jax.ShapeDtypeStruct(keys.shape, bf),
            jax.ShapeDtypeStruct(keys.shape, bf),
            jax.ShapeDtypeStruct(wgv.shape, f32),
            jax.ShapeDtypeStruct(wgo.shape, f32),
        ),
        in_specs=[pl.BlockSpec(memory_space=pltpu.SMEM), vmem, vmem, vmem] + [hbm] * 4,
        out_specs=[hbm] * 4,
        scratch_shapes=[
            pltpu.VMEM(keys.shape, bf), pltpu.VMEM(keys.shape, bf),
            pltpu.VMEM(keys.shape, bf), pltpu.VMEM(keys.shape, bf),
            pltpu.VMEM((npair, BLK, WIN), f32), pltpu.VMEM((npair, BLK, WIN), f32),
            pltpu.VMEM((nwin + 1, 2 * WIN, 2 * HD), bf),
            pltpu.VMEM((8, total + WIN), f32), pltpu.VMEM((8, total + WIN), f32),
            pltpu.VMEM((2,) + wgv.shape, f32),
            dma((nchunk,)), dma((nchunk,)), dma((nchunk,)), dma((nchunk,)), dma((4,)),
        ],
        compiler_params=pltpu.CompilerParams(vmem_limit_bytes=60 * 1024 * 1024),
    )(tab, bounds, g, q, wgv, wgo, keys, values)


def on_device_kernels(
    ndp, nt, patch_states, residual_grad, upstream_value, norm_gain, value_weight, out_weight,
    attn_out, queries, byte_keys, byte_values, patch_starts,
):
    nbytes = byte_keys.shape[1]
    wgv, wgo, g, q, tab, bounds = grad_call(
        ndp, nt, nbytes, patch_states[0], residual_grad[0], upstream_value[0],
        norm_gain.reshape(-1, 128), value_weight, out_weight, attn_out[0], queries[0], patch_starts,
    )
    gk, gv, wgv, wgo = byte_call(
        tab, bounds, g.reshape(-1, HD), q.reshape(-1, HD), wgv, wgo.reshape(wgv.shape), byte_keys[0], byte_values[0]
    )
    return (wgv, wgo, gk[None], gv[None])


def solution(mesh):
    ndp, nseq, nt = mesh.shape["dp"], mesh.shape["seq"], mesh.shape["tensor"]
    use_kernels = nseq == 2 and ndp == 4
    body = functools.partial(on_device_kernels, ndp, nt) if use_kernels else on_device
    return jax.shard_map(
        body,
        mesh=mesh,
        in_specs=(
            P("dp", "seq", "tensor"),
            P("dp", "seq", "tensor"),
            P("dp", "seq", None),
            P("tensor"),
            P(("dp", "seq"), "tensor"),
            P(("dp", "seq"), "tensor"),
            P("dp", "seq", None),
            P("dp", "seq", "tensor"),
            P("dp", "seq", "tensor"),
            P("dp", "seq", "tensor"),
            P("dp", None),
        ),
        out_specs=(
            P(("dp", "seq"), "tensor"),
            P(("dp", "seq"), "tensor"),
            P("dp", "seq", "tensor"),
            P("dp", "seq", "tensor"),
        ),
        check_vma=False,
    )
```

```python
import functools
import math

import jax
import jax.numpy as jnp
from jax import lax
from jax.experimental import pallas as pl
from jax.experimental.pallas import tpu as pltpu
from jax.sharding import PartitionSpec as P

HD = 128


def member_sum(member32, terms):
    return lax.dot_general(
        member32,
        terms,
        (((0,), (0,)), ((), ())),
        precision=lax.Precision.HIGHEST,
        preferred_element_type=jnp.float32,
    )


def member_spread(member32, totals):
    return jnp.dot(
        member32, totals, precision=lax.Precision.HIGHEST, preferred_element_type=jnp.float32
    )


def cross_backward(member, segment_rows, keys, values, head_width):
    nbytes = keys.shape[0]
    heads = keys.shape[1] // HD
    scale = 1.0 / math.sqrt(HD)
    member32 = member.astype(jnp.float32)
    picked = jnp.dot(member, segment_rows, preferred_element_type=jnp.float32).astype(jnp.bfloat16)
    grad_f = picked[:, :head_width].astype(jnp.float32).reshape(nbytes, heads, HD)
    query_f = picked[:, head_width:].astype(jnp.float32).reshape(nbytes, heads, HD)
    keys_f = keys.astype(jnp.float32).reshape(nbytes, heads, HD)
    values_f = values.astype(jnp.float32).reshape(nbytes, heads, HD)
    scores = jnp.sum(query_f * keys_f, axis=-1) * scale
    expo = jnp.exp(scores)
    totals = member_spread(member32, member_sum(member32, expo))
    probs = expo / totals
    grad_values = (probs[..., None] * grad_f).reshape(nbytes, heads * HD).astype(jnp.bfloat16)
    prob_grad = jnp.sum(grad_f * values_f, axis=-1)
    mass = member_spread(member32, member_sum(member32, probs * prob_grad))
    score_grad = probs * (prob_grad - mass)
    grad_keys = (
        (score_grad[..., None] * query_f * scale).reshape(nbytes, heads * HD).astype(jnp.bfloat16)
    )
    return (grad_keys, grad_values)


def contract_rows(left, right):
    return lax.dot_general(
        left, right, (((0,), (0,)), ((), ())), preferred_element_type=jnp.float32
    )


def on_device(
    patch_states,
    residual_grad,
    upstream_value,
    norm_gain,
    value_weight,
    out_weight,
    attn_out,
    queries,
    byte_keys,
    byte_values,
    patch_starts,
):
    states = patch_states[0]
    patches = states.shape[0]
    width_local = states.shape[1]
    model_width = width_local * lax.axis_size("tensor")
    states32 = states.astype(jnp.float32)
    gain32 = norm_gain.astype(jnp.float32)
    upstream = upstream_value[0]
    context = attn_out[0]
    value_full, out_full = (
        lax.all_gather(value_weight, ("dp", "seq"), axis=0, tiled=True),
        lax.all_gather(out_weight, ("dp", "seq"), axis=0, tiled=True),
    )
    grad_normed = jnp.dot(upstream, value_full, preferred_element_type=jnp.float32)
    square_part = jnp.sum(states32 * states32, axis=1)
    cross_part = jnp.sum(grad_normed * gain32 * states32, axis=1)
    square_sum, cross_sum = lax.psum((square_part, cross_part), "tensor")
    inv_rms = lax.rsqrt(square_sum / model_width + 1e-05)
    normed = (states32 * inv_rms[:, None] * gain32).astype(jnp.bfloat16)
    grad_patch = (
        residual_grad[0].astype(jnp.float32)
        + inv_rms[:, None] * gain32 * grad_normed
        - (inv_rms**3)[:, None] * states32 * (cross_sum / model_width)[:, None]
    ).astype(jnp.bfloat16)
    partial_attn = lax.dot_general(
        grad_patch, out_full, (((1,), (1,)), ((), ())), preferred_element_type=jnp.float32
    )
    columns = upstream
    wgrad_value = lax.psum_scatter(
        contract_rows(columns, normed), ("dp", "seq"), scatter_dimension=0, tiled=True
    )
    columns = context
    wgrad_out = lax.psum_scatter(
        contract_rows(columns, grad_patch), ("dp", "seq"), scatter_dimension=0, tiled=True
    )
    attn_all = lax.psum(partial_attn, "tensor").astype(jnp.bfloat16)
    head_width = queries.shape[2]
    grad_attn = lax.dynamic_slice_in_dim(
        attn_all, lax.axis_index("tensor") * head_width, head_width, 1
    )
    starts = patch_starts[0]
    total_patches = starts.shape[0]
    seq_count = lax.axis_size("seq")
    seq_pos = lax.axis_index("seq")
    byte_count = byte_keys.shape[1]
    window_len = 2 * patches
    owners = starts // byte_count
    shard_ids = jnp.arange(seq_count, dtype=jnp.int32)
    firsts = jnp.sum((owners[None, :] < shard_ids[:, None]).astype(jnp.int32), axis=1)
    my_first = jnp.sum(firsts * (shard_ids == seq_pos).astype(jnp.int32))
    payload = jnp.concatenate([grad_attn, queries[0]], axis=1)
    padded_starts = jnp.concatenate(
        [starts, jnp.full((window_len,), 2 * total_patches * byte_count + byte_count, jnp.int32)]
    )
    local_starts = lax.dynamic_slice_in_dim(padded_starts, my_first, window_len)
    positions = seq_pos * byte_count + jnp.arange(byte_count, dtype=jnp.int32)
    reached = local_starts[None, :] <= positions[:, None]
    after = jnp.concatenate([reached[:, 1:], jnp.zeros((byte_count, 1), bool)], axis=1)
    member = (reached & jnp.logical_not(after)).astype(jnp.bfloat16)
    mine = seq_pos * patches + jnp.arange(patches, dtype=jnp.int32)
    targets = lax.dynamic_slice_in_dim(owners, seq_pos * patches, patches)
    target_first = jnp.sum((owners[None, :] < targets[:, None]).astype(jnp.int32), axis=1)
    slots = mine - jnp.maximum(seq_pos * patches, target_first)
    dest = targets * patches + slots
    place = (jnp.arange(seq_count * patches, dtype=jnp.int32)[:, None] == dest[None, :]).astype(
        jnp.bfloat16
    )
    outgoing = jnp.dot(place, payload, preferred_element_type=jnp.float32).astype(jnp.bfloat16)
    outgoing = outgoing.reshape(seq_count, patches, 2 * head_width)
    incoming = lax.all_to_all(outgoing, "seq", split_axis=0, concat_axis=0, tiled=True)
    wanted = my_first + jnp.arange(window_len, dtype=jnp.int32)
    sources = wanted // patches
    received_row = sources * patches + wanted - jnp.maximum(sources * patches, my_first)
    select = (
        received_row[:, None] == jnp.arange(seq_count * patches, dtype=jnp.int32)[None, :]
    ).astype(jnp.bfloat16)
    segment_rows = jnp.dot(
        select,
        incoming.reshape(seq_count * patches, 2 * head_width),
        preferred_element_type=jnp.float32,
    ).astype(jnp.bfloat16)
    grad_keys, grad_values = cross_backward(
        member, segment_rows, byte_keys[0], byte_values[0], head_width
    )
    return (wgrad_value, wgrad_out, grad_keys[None], grad_values[None])


BLK = 256
GROUP = 8
WIN = 128


def tile_terms(b, w, keys, values, bd, bounds):
    both = jnp.concatenate([keys[b], values[b]], axis=1)
    s = lax.dot_general(both, bd[w], (((1,), (1,)), ((), ())), preferred_element_type=jnp.float32)
    row = lax.broadcasted_iota(jnp.int32, (BLK, WIN), 0) + b * BLK
    limits = bounds[w]
    inside = (row >= limits[0:1, :]) & (row < limits[1:2, :])
    return jnp.where(inside, jnp.exp(s[:, :WIN] * (1.0 / math.sqrt(HD))), 0.0), s[:, WIN:]


def grad_kernel(
    ndp, nt, nbytes, states_in, resid_in, up_in, gain_in, vw, ow, ctx_in, q_in, starts,
    keys_in, values_in, wgv, wgo, bd_out, e_out, p_out, tab, table, means,
    states, resid, up, ctx, gain, wall, sqs, sqr, part, acc, acco, accz, rbz, lbz, ysz, yrz, rbv, lbv, ysv, yrv, rbo, lbo, yso, yro,
    pas, par, gn, nrm, gpat, trans_v, trans_o, gsend, gboth, qboth, keys, values, bd, bounds, expo, pgrad, psums, tab_s,
    s_in, s_e, s_p, s_out, s_ag, r_ag, s_sq, r_sq, s_rv, r_rv, s_lv, r_lv, s_ro, r_ro, s_lo, r_lo,
    s_rz, r_rz, s_lz, r_lz, s_yo, r_yo, s_yv, r_yv, s_pa, r_pa, s_g, r_g,
):
    dp, sq, tn = lax.axis_index("dp"), lax.axis_index("seq"), lax.axis_index("tensor")
    patches, width = states.shape
    model = width * nt
    last = ndp - 1
    mine = dp * 2 + sq
    tall = 128
    nrow = patches // tall
    ncol = width // 256

    right, left = (dp + 1, sq, tn), (dp - 1, sq, tn)
    ydev = (dp, 1 - sq, tn)

    def tdev(k):
        return (dp, sq, lax.rem(tn + k, nt))

    def copy(src, dst, ssem, rsem, dev):
        return pltpu.make_async_remote_copy(
            src_ref=src, dst_ref=dst, send_sem=ssem, recv_sem=rsem,
            device_id=dev, device_id_type=pl.DeviceIdType.MESH,
        )

    local = {}
    for i, (name, src, dst) in enumerate(
        (("states", states_in, states), ("up", up_in, up), ("resid", resid_in, resid),
         ("ctx", ctx_in, ctx), ("q", q_in, qboth.at[sq]), ("vw", vw, wall.at[0, mine]),
         ("ow", ow, wall.at[1, mine]), ("keys", keys_in, keys), ("values", values_in, values))
    ):
        local[name] = pltpu.make_async_copy(src, dst, s_in.at[i])
        local[name].start()

    barrier = pltpu.get_barrier_semaphore()
    peers = [(lax.rem(dp + k, ndp), sq, tn) for k in range(1, ndp)]
    peers += [tdev(k) for k in range(1, nt)] + [ydev]
    for dev in peers:
        pl.semaphore_signal(barrier, inc=1, device_id=dev, device_id_type=pl.DeviceIdType.MESH)
    pl.semaphore_wait(barrier, len(peers))

    sent = []

    def go(c, cond=None):
        if cond is None:
            c.start()
        else:
            pl.when(cond)(c.start)
        sent.append((c, cond))
        return c

    weights = (vw, ow)

    def half(h):
        return pl.ds(h * (vw.shape[0] // 2), vw.shape[0] // 2)

    def shard(w, zz, yy, h, dev, k, own=False):
        slot = zz * 2 + yy
        block = wall.at[w, slot, half(h)]
        src = weights[w].at[half(h)] if own else block
        return copy(src, block, s_ag.at[w, h, k], r_ag.at[w, h, slot], dev)

    def ag_own_z(w, h, ends=True, inner=True):
        for dev, onward, edge, k in ((right, dp < last, dp == 0, 0), (left, dp > 0, dp == last, 1)):
            if ends:
                go(shard(w, dp, sq, h, dev, k, True), edge)
            if inner:
                go(shard(w, dp, sq, h, dev, k, True), onward & jnp.logical_not(edge))

    def ag_own_y(w, h):
        go(shard(w, dp, sq, h, ydev, 2, True))

    def ag_forward(w, s, h):
        for zz, here, dev, onward, k in (
            (dp - s, dp - s >= 0, right, dp < last, 3 * s),
            (dp + s, dp + s <= last, left, dp > 0, 3 * ndp + 3 * s),
        ):
            pl.when(here)(shard(w, zz, sq, h, dev, k).wait_recv)
            go(shard(w, zz, sq, h, dev, k), here & onward)
            spread = here if w == 0 or s > 1 else here & ((zz == 0) | (zz == last))
            go(shard(w, zz, sq, h, ydev, k + 1), spread)

    def ag_cross(w, h):
        inner = (dp > 0) & (dp < last)
        pl.when(inner)(shard(w, dp, 1 - sq, h, ydev, 2).wait_recv)
        go(shard(w, dp, 1 - sq, h, right, 11), inner)
        go(shard(w, dp, 1 - sq, h, left, 12), inner)

    def ag_wait_y(w):
        for zz in range(ndp):
            for h in range(2):
                wait = shard(w, zz, 1 - sq, h, ydev, 2).wait_recv
                if w == 0 or zz in (0, last):
                    wait()
                else:
                    pl.when(dp != zz)(wait)

    def row_loop(fn):
        def body(i, _):
            fn(pl.ds(pl.multiple_of(i * tall, tall), tall), i)
            return 0

        lax.fori_loop(0, nrow, body, 0)

    def to_row(col):
        return jnp.broadcast_to(col, (tall, 128)).T[:8]

    def share(which):
        return [
            go(copy(sqs.at[which], sqr.at[which, k - 1], s_sq.at[which, k - 1],
                    r_sq.at[which, k - 1], tdev(k)))
            for k in range(1, nt)
        ]

    def total_col(which, i):
        rows = sqs[which, i]
        for k in range(nt - 1):
            rows = rows + sqr[which, k, i]
        return jnp.broadcast_to(rows[0:1, :], (128, tall)).T[:, 0:1]

    def inverse(i):
        return lax.rsqrt(total_col(0, i) / model + 1e-05)

    def square(here, i):
        x = states[here, :].astype(jnp.float32)
        sqs[0, i] = to_row(jnp.sum(x * x, axis=1, keepdims=True))

    def normalise(here, i):
        x = states[here, :].astype(jnp.float32)
        nrm[here, :] = (x * inverse(i) * gain[0:1, :]).astype(jnp.bfloat16)

    def wgrad(w, trans, factor):
        nblk, rows_per = part.shape[1], part.shape[2]

        def body(c, _):
            cols = pl.ds(pl.multiple_of(c * 256, 256), 256)
            out = jnp.dot(trans[...], factor[:, cols], preferred_element_type=jnp.float32)
            part[w, :, :, cols] = out.reshape(nblk, rows_per, 256)
            return 0

        lax.fori_loop(0, ncol, body, 0)

    def part_v(zz, h):
        return part[0, zz * 2 + h]

    def part_z(zz, h):
        return part[1, zz * 2 + h, half(1)]

    def part_o(zz, h):
        yo(zz, h).wait_recv()
        return part[1, zz * 2 + sq, half(h)] + yro[zz, h].astype(jnp.float32)

    def hops(d, h, buf_r, buf_l, s_r, r_r, s_l, r_l):
        for zz, valid, dev, fed, buf, ss, rs in (
            (dp + d, dp + d <= last, right, dp > 0, buf_r, s_r, r_r),
            (dp - d, dp - d >= 0, left, dp < last, buf_l, s_l, r_l),
        ):
            c = copy(buf.at[zz, h], buf.at[zz, h], ss.at[d - 1, h], rs.at[zz, h], dev)
            yield zz, valid, fed, buf, c

    def line_open(get, bufs, halves=(0, 1)):
        for d in range(last, 0, -1):
            for h in halves:
                for zz, valid, fed, buf, c in hops(d, h, *bufs):
                    opening = valid & jnp.logical_not(fed)

                    @pl.when(opening)
                    def _(zz=zz, h=h, buf=buf):
                        buf[zz, h] = get(zz, h).astype(jnp.bfloat16)

                    go(c, opening)

    def line(d, h, get, bufs):
        for zz, valid, fed, buf, c in hops(d, h, *bufs):

            @pl.when(valid & fed)
            def _(zz=zz, buf=buf, c=c):
                mine_part = get(zz, h)
                c.wait_recv()
                buf[zz, h] = (mine_part + buf[zz, h].astype(jnp.float32)).astype(jnp.bfloat16)

            go(c, valid & fed)

    def line_end(h, acc, bufs):
        buf_r, buf_l, s_r, r_r, s_l, r_l = bufs
        for fed, dev, buf, ss, rs in (
            (dp > 0, right, buf_r, s_r, r_r),
            (dp < last, left, buf_l, s_l, r_l),
        ):
            c = copy(buf.at[dp, h], buf.at[dp, h], ss.at[0, h], rs.at[dp, h], dev)

            @pl.when(fed)
            def _(c=c, buf=buf):
                c.wait_recv()
                acc[h] += buf[dp, h].astype(jnp.float32)

    line_v = (rbv, lbv, s_rv, r_rv, s_lv, r_lv)
    line_o = (rbo, lbo, s_ro, r_ro, s_lo, r_lo)
    line_z = (rbz, lbz, s_rz, r_rz, s_lz, r_lz)

    def yo(zz, h):
        return copy(yso.at[zz, h], yro.at[zz, h], s_yo.at[zz, h], r_yo.at[zz, h], ydev)

    def send_yo(zz, h, cond=None):
        def fill():
            yso[zz, h] = part[1, zz * 2 + (1 - sq), half(h)].astype(jnp.bfloat16)

        fill() if cond is None else pl.when(cond)(fill)
        go(yo(zz, h), cond)

    for h in range(2):
        ag_own_z(0, h)
        ag_own_y(0, h)
    for i in range(width // 128):
        gain[:, i * 128 : (i + 1) * 128] = jnp.broadcast_to(
            gain_in[i : i + 1, :].astype(jnp.float32), (8, 128)
        )
    local["states"].wait()
    row_loop(square)
    sq_copies = share(0)
    local["up"].wait()
    trans_v[...] = up[...].T

    first = starts[0:1, :] - sq * nbytes
    row8 = jnp.broadcast_to(first, (8, first.shape[1]))
    lane = lax.broadcasted_iota(jnp.int32, row8.shape, 1)
    after = jnp.where(
        lane == first.shape[1] - 1, 2 * nbytes, pltpu.roll(row8, first.shape[1] - 1, 1)
    )
    for w in range(first.shape[1] // WIN):
        lanes = slice(w * WIN, (w + 1) * WIN)
        bounds[w, 0:1, :] = first[:, lanes]
        bounds[w, 1:2, :] = after[0:1, lanes]
    bounds[first.shape[1] // WIN] = jnp.full(bounds.shape[1:], 4 * nbytes, jnp.int32)

    ag_forward(0, 1, 0)
    for h in range(2):
        ag_own_z(1, h, inner=False)
    for c in sq_copies:
        c.wait_recv()
    row_loop(normalise)
    ag_forward(0, 1, 1)
    wgrad(0, trans_v, nrm)
    line_open(part_v, line_v)
    ag_forward(0, 2, 0)
    nblocks = nbytes // BLK
    ends = lax.broadcasted_iota(jnp.int32, (nblocks, first.shape[1]), 0) * BLK + (BLK - 1)
    reach = (jnp.broadcast_to(first, ends.shape) <= ends).astype(jnp.int32)
    high = (jnp.sum(reach, axis=1, keepdims=True) - 1) // WIN
    low = (jnp.sum((first <= 0).astype(jnp.int32), axis=1, keepdims=True) - 1) // WIN
    step = lax.broadcasted_iota(jnp.int32, (nblocks, 128), 0) + high - low
    pair = lax.broadcasted_iota(jnp.int32, (nblocks, 128), 1)
    block_of = jnp.sum((step < pair).astype(jnp.int32), axis=0, keepdims=True)
    window = lax.broadcasted_iota(jnp.int32, (1, 128), 1) - block_of + low
    done = block_of >= nblocks
    tab[0:1, :] = jnp.where(done, nblocks - 1, block_of)
    nwin = first.shape[1] // WIN
    window = jnp.where(done, nwin, window)
    tab[1:2, :] = window
    window_of = jnp.broadcast_to(window.astype(jnp.float32), (128, 128)).T[: psums.shape[1], 0:1]
    local["tab"] = pltpu.make_async_copy(tab, tab_s, s_in.at[9])
    local["tab"].start()
    for w in range(nwin):
        bd[w, :WIN, HD:] = jnp.zeros((WIN, HD), jnp.bfloat16)
        bd[w, WIN:, :HD] = jnp.zeros((WIN, HD), jnp.bfloat16)
    bd[nwin] = jnp.zeros(bd.shape[1:], jnp.bfloat16)

    ag_forward(0, 2, 1)
    local["ctx"].wait()
    trans_o[...] = ctx[...].T
    for h in range(2):
        ag_forward(0, 3, h)
        ag_own_z(1, h, ends=False)
        ag_own_y(1, h)
    ag_forward(1, 1, 0)
    local["vw"].wait()
    ag_wait_y(0)
    ag_forward(1, 1, 1)

    def project(here, i):
        full = wall[0].reshape(up.shape[1], width)
        g = jnp.dot(up[here, :], full, preferred_element_type=jnp.float32)
        gn[here, :] = g
        x = states[here, :].astype(jnp.float32)
        sqs[1, i] = to_row(jnp.sum(g * gain[0:1, :] * x, axis=1, keepdims=True))

    row_loop(project)
    cr_copies = share(1)
    ag_cross(1, 0)
    ag_forward(1, 2, 0)
    ag_cross(1, 1)
    line(2, 0, part_v, line_v)
    ag_forward(1, 2, 1)
    line(2, 1, part_v, line_v)
    local["resid"].wait()
    for c in cr_copies:
        c.wait_recv()

    def make_grad(here, i):
        inv = inverse(i)
        cross = total_col(1, i) / model
        x = states[here, :].astype(jnp.float32)
        gpat[here, :] = (
            resid[here, :].astype(jnp.float32)
            + inv * gain[0:1, :] * gn[here, :]
            - (inv * inv * inv * cross) * x
        ).astype(jnp.bfloat16)

    row_loop(make_grad)
    ag_forward(1, 3, 0)
    ag_forward(1, 3, 1)
    local["q"].wait()
    qc = go(copy(qboth.at[sq], qboth.at[sq], s_g.at[0], r_g.at[0], ydev))
    wgrad(1, trans_o, gpat)
    line_open(part_z, line_z)
    for k in range(ndp - 1, 0, -1):
        send_yo(dp + k, 0, dp + k <= last)
        send_yo(dp - k, 0, dp - k >= 0)
    send_yo(dp, 0)
    for h in range(2):
        line(1, h, part_v, line_v)
    for h in range(2):
        line(2, h, part_z, line_z)
    local["ow"].wait()
    ag_wait_y(1)

    def tile(i):
        return pl.ds(i * tall, tall)

    def pa(i, k):
        return copy(gsend.at[k - 1, tile(i)], par.at[k - 1, tile(i)], s_pa.at[k - 1, i],
                    r_pa.at[k - 1, i], tdev(k))

    for i in range(nrow):
        full = wall[1].reshape(up.shape[1], width)
        p = lax.dot_general(
            gpat[tile(i), :], full, (((1,), (1,)), ((), ())), preferred_element_type=jnp.float32
        )
        for j in range(nt):
            pas[j, tile(i), :] = p[:, j * HD : (j + 1) * HD]
        for k in range(1, nt):
            gsend[k - 1, tile(i)] = pas[lax.rem(tn + k, nt), tile(i)].astype(jnp.bfloat16)
            go(pa(i, k))

    for h in range(2):
        acc[h] = part_v(dp, h)
        line_end(h, acc, line_v)
    ysv[...] = acc[1 - sq].astype(jnp.bfloat16)
    yv = go(copy(ysv, yrv, s_yv.at[0], r_yv.at[0], ydev))
    line_open(part_o, line_o, (0,))
    for h in range(2):
        line(1, h, part_z, line_z)
    line(2, 0, part_o, line_o)
    gc = []
    for i in range(nrow):
        total = pas[tn, tile(i)]
        for k in range(1, nt):
            pa(i, k).wait_recv()
            total = total + par[k - 1, tile(i)].astype(jnp.float32)
        gboth[sq, tile(i)] = total.astype(jnp.bfloat16)
        block = gboth.at[sq, tile(i)]
        gc.append(go(copy(block, block, s_g.at[1 + i], r_g.at[1 + i], ydev)))
    for h in range(2):
        accz[h] = part_z(dp, h)
        line_end(h, accz, line_z)
    ysz[...] = accz[1 - sq].astype(jnp.bfloat16)
    yz = go(copy(ysz, yrz, s_yv.at[1], r_yv.at[1], ydev))
    ngroup = psums.shape[1] // GROUP

    def terms(group):
        here = pl.ds(group * GROUP, GROUP)
        return (
            pltpu.make_async_copy(expo.at[here], e_out.at[here], s_e.at[group]),
            pltpu.make_async_copy(pgrad.at[here], p_out.at[here], s_p.at[group]),
        )

    def measure(group, _):
        for k in range(GROUP):
            n = group * GROUP + k
            e, pg = tile_terms(tab_s[0, n], tab_s[1, n], keys, values, bd, bounds)
            expo[n] = e.astype(jnp.bfloat16)
            t = jnp.sum(e, axis=0, keepdims=True)
            m = jnp.sum(e * pg, axis=0, keepdims=True)
            mean = m / jnp.where(t > 0.0, t, 1.0)
            pgrad[n] = (pg - mean).astype(jnp.bfloat16)
            psums[0, pl.ds(n, 1), :] = t
            psums[1, pl.ds(n, 1), :] = m
            means[pl.ds(n, 1), :] = mean
        for c in terms(group):
            c.start()
        return 0

    line(1, 0, part_o, line_o)
    yv.wait_recv()
    acc[0] = acc[sq] + yrv[...].astype(jnp.float32)
    out_v = pltpu.make_async_copy(acc.at[0], wgv, s_out.at[0])
    out_v.start()
    qc.wait_recv()
    for c in gc:
        c.wait_recv()
    for w in range(nwin):
        at = (w * WIN // patches, pl.ds(w * WIN % patches, WIN))
        bd[w, :WIN, :HD] = qboth[at]
        bd[w, WIN:, HD:] = gboth[at]
    out_bd = pltpu.make_async_copy(bd, bd_out, s_out.at[2])
    out_bd.start()
    for name in ("keys", "values", "tab"):
        local[name].wait()
    lax.fori_loop(0, ngroup, measure, 0)
    for w in range(nwin):
        lanes = slice(w * WIN, (w + 1) * WIN)
        here = window_of == float(w)
        t = jnp.sum(jnp.where(here, psums[0], 0.0), axis=0, keepdims=True)
        m = jnp.sum(jnp.where(here, psums[1], 0.0), axis=0, keepdims=True)
        inv = jnp.where(t > 0.0, 1.0 / jnp.where(t > 0.0, t, 1.0), 0.0)
        table[0:1, lanes] = inv
        table[1:2, lanes] = m * inv
    table[:, nwin * WIN :] = jnp.zeros((2, WIN), jnp.float32)
    acco[0] = part_o(dp, 0)
    line_end(0, acco, line_o)
    yz.wait_recv()
    acco[1] = accz[sq] + yrz[...].astype(jnp.float32)
    out_o = pltpu.make_async_copy(acco, wgo, s_out.at[1])
    out_o.start()
    for group in range(ngroup):
        for c in terms(group):
            c.wait()
    for c, cond in sent:
        if cond is None:
            c.wait_send()
        else:
            pl.when(cond)(c.wait_send)
    for c in (out_v, out_o, out_bd):
        c.wait()


def grad_call(ndp, nt, states, resid, up, gain, vw, ow, ctx, q, starts, keys, values):
    patches, width = states.shape
    rows = vw.shape[0]
    nblk = 2 * ndp
    nk = up.shape[1]
    bf, f32, i32 = jnp.bfloat16, jnp.float32, jnp.int32
    nrow = patches // 128
    nbytes = keys.shape[0] * BLK
    total = starts.shape[1]
    nwin = total // WIN
    npair = -(-(nbytes // BLK + nwin - 1) // GROUP) * GROUP
    vmem = pl.BlockSpec(memory_space=pltpu.VMEM)
    hbm = pl.BlockSpec(memory_space=pl.ANY)
    dma = pltpu.SemaphoreType.DMA
    return pl.pallas_call(
        functools.partial(grad_kernel, ndp, nt, nbytes),
        out_shape=(
            jax.ShapeDtypeStruct((rows, width), f32),
            jax.ShapeDtypeStruct((2, rows // 2, width), f32),
            jax.ShapeDtypeStruct((nwin + 1, 2 * WIN, 2 * HD), bf),
            jax.ShapeDtypeStruct((npair, BLK, WIN), bf),
            jax.ShapeDtypeStruct((npair, BLK, WIN), bf),
            jax.ShapeDtypeStruct((2, 128), i32),
            jax.ShapeDtypeStruct((2, total + WIN), f32),
            jax.ShapeDtypeStruct((npair, WIN), f32),
        ),
        in_specs=[hbm, hbm, hbm, vmem, hbm, hbm, hbm, hbm, vmem, hbm, hbm],
        out_specs=[hbm] * 5 + [vmem] * 3,
        scratch_shapes=[
            pltpu.VMEM((patches, width), bf),
            pltpu.VMEM((patches, width), bf),
            pltpu.VMEM((patches, nk), bf),
            pltpu.VMEM((patches, nk), bf),
            pltpu.VMEM((8, width), f32),
            pltpu.VMEM((2, nblk, rows, width), bf),
            pltpu.VMEM((2, nrow, 8, 128), f32),
            pltpu.VMEM((2, nt - 1, nrow, 8, 128), f32),
            pltpu.VMEM((2, nblk, rows, width), f32),
            pltpu.VMEM((2, rows, width), f32),
            pltpu.VMEM((2, rows // 2, width), f32),
            pltpu.VMEM((2, rows // 2, width), f32),
            pltpu.VMEM((ndp, 2, rows // 2, width), bf),
            pltpu.VMEM((ndp, 2, rows // 2, width), bf),
            pltpu.VMEM((rows // 2, width), bf),
            pltpu.VMEM((rows // 2, width), bf),
            pltpu.VMEM((ndp, 2, rows, width), bf),
            pltpu.VMEM((ndp, 2, rows, width), bf),
            pltpu.VMEM((rows, width), bf),
            pltpu.VMEM((rows, width), bf),
            pltpu.VMEM((ndp, 2, rows // 2, width), bf),
            pltpu.VMEM((ndp, 2, rows // 2, width), bf),
            pltpu.VMEM((ndp, 2, rows // 2, width), bf),
            pltpu.VMEM((ndp, 2, rows // 2, width), bf),
            pltpu.VMEM((nt, patches, HD), f32),
            pltpu.VMEM((nt - 1, patches, HD), bf),
            pltpu.VMEM((patches, width), f32),
            pltpu.VMEM((patches, width), bf),
            pltpu.VMEM((patches, width), bf),
            pltpu.VMEM((nk, patches), bf),
            pltpu.VMEM((nk, patches), bf),
            pltpu.VMEM((nt - 1, patches, HD), bf),
            pltpu.VMEM((2, patches, HD), bf),
            pltpu.VMEM((2, patches, HD), bf),
            pltpu.VMEM(keys.shape, bf),
            pltpu.VMEM(keys.shape, bf),
            pltpu.VMEM((nwin + 1, 2 * WIN, 2 * HD), bf),
            pltpu.VMEM((nwin + 1, 2, WIN), i32),
            pltpu.VMEM((npair, BLK, WIN), bf),
            pltpu.VMEM((npair, BLK, WIN), bf),
            pltpu.VMEM((2, npair, WIN), f32),
            pltpu.SMEM((2, 128), i32),
            dma((10,)), dma((npair // GROUP,)), dma((npair // GROUP,)), dma((3,)),
            dma((2, 2, 6 * ndp)), dma((2, 2, nblk)),
            dma((2, nt - 1)), dma((2, nt - 1)),
            dma((ndp, 2)), dma((ndp, 2)), dma((ndp, 2)), dma((ndp, 2)),
            dma((ndp, 2)), dma((ndp, 2)), dma((ndp, 2)), dma((ndp, 2)),
            dma((ndp, 2)), dma((ndp, 2)), dma((ndp, 2)), dma((ndp, 2)),
            dma((ndp, 2)), dma((ndp, 2)), dma((2,)), dma((2,)),
            dma((nt - 1, nrow)), dma((nt - 1, nrow)), dma((1 + nrow,)), dma((1 + nrow,)),
        ],
        compiler_params=pltpu.CompilerParams(
            collective_id=0, has_side_effects=True, vmem_limit_bytes=60 * 1024 * 1024
        ),
    )(states, resid, up, gain, vw, ow, ctx, q, starts, keys, values)


def byte_kernel(
    tab_in, table_in, means_in, bd_in, e_in, p_in, wgv_in, wgo_in, gk_out, gv_out, wgv, wgo,
    tab, table, means, bd, expo, pgrad, gk, gv, held, s_e, s_p, o_k, o_v, s_w, s_t,
):
    nwin = bd.shape[0] - 1
    nbytes = gk.shape[0]
    ngroup = expo.shape[0] // GROUP
    nchunk = o_k.shape[0]
    chunk = nbytes // nchunk
    ready = GROUP * BLK // chunk
    behind = -(-(nwin - 1) // (chunk // BLK))
    scale = 1.0 / math.sqrt(HD)

    def load(c):
        here = pl.ds(c * GROUP, GROUP)
        return (
            pltpu.make_async_copy(e_in.at[here], expo.at[here], s_e.at[c]),
            pltpu.make_async_copy(p_in.at[here], pgrad.at[here], s_p.at[c]),
        )

    def store(c):
        here = pl.ds(pl.multiple_of(c * chunk, chunk), chunk)
        return (
            pltpu.make_async_copy(gk.at[here], gk_out.at[here], o_k.at[c]),
            pltpu.make_async_copy(gv.at[here], gv_out.at[here], o_v.at[c]),
        )

    small = [
        pltpu.make_async_copy(a, b, s_t.at[i])
        for i, (a, b) in enumerate((
            (tab_in, tab), (table_in, table), (means_in, means), (bd_in, bd)
        ))
    ]
    for x in small:
        x.start()
    for c in range(ngroup):
        for x in load(c):
            x.start()
    carried = ((wgv_in, wgv), (wgo_in, wgo))
    taken = [pltpu.make_async_copy(a, held.at[i], s_w.at[i]) for i, (a, _) in enumerate(carried)]
    passed = [pltpu.make_async_copy(held.at[i], b, s_w.at[2 + i]) for i, (_, b) in enumerate(carried)]
    for x in taken:
        x.start()
    for x in small:
        x.wait()

    def apply(group, _):
        for x in load(group):
            x.wait()
        first = group * GROUP
        prior = jnp.maximum(first - 1, 0)
        before = pl.ds(pl.multiple_of(tab[0, prior] * BLK, BLK), BLK)
        held_k, held_v = gk[before, :], gv[before, :]
        for k in range(GROUP):
            n = first + k
            b, w = tab[0, n], tab[1, n]
            here = pl.ds(pl.multiple_of(b * BLK, BLK), BLK)
            lanes = pl.ds(pl.multiple_of(w * WIN, WIN), WIN)
            same = tab[0, jnp.maximum(n - 1, 0)] == b
            same = same & (n > 0) if k == 0 else same
            p = expo[n].astype(jnp.float32) * table[0:1, lanes]
            shift = means[pl.ds(n, 1), :] - table[1:2, lanes]
            sg = p * (pgrad[n].astype(jnp.float32) + shift) * scale
            both = jnp.concatenate([sg.astype(jnp.bfloat16), p.astype(jnp.bfloat16)], axis=1)
            out = jnp.dot(both, bd[w], preferred_element_type=jnp.float32).astype(jnp.bfloat16)
            held_k = out[:, :HD] + jnp.where(same, held_k, jnp.zeros_like(held_k))
            held_v = out[:, HD:] + jnp.where(same, held_v, jnp.zeros_like(held_v))
            gk[here, :] = held_k
            gv[here, :] = held_v

        for r in range(ready):
            done = group * ready + r - behind

            @pl.when((done >= 0) & (done < nchunk))
            def _(done=done):
                for x in store(done):
                    x.start()

        return 0

    lax.fori_loop(0, ngroup, apply, 0)
    for x, y in zip(taken, passed):
        x.wait()
        y.start()
    for c in range(max(ngroup * ready - behind, 0), nchunk):
        for x in store(c):
            x.start()
    for c in range(nchunk):
        for x in store(c):
            x.wait()
    for x in passed:
        x.wait()


def byte_call(tab, table, means, bd, expo, pgrad, wgv, wgo, out):
    bf, f32 = jnp.bfloat16, jnp.float32
    nchunk = out.shape[0] // 1024
    ngroup = expo.shape[0] // GROUP
    hbm = pl.BlockSpec(memory_space=pl.ANY)
    dma = pltpu.SemaphoreType.DMA
    return pl.pallas_call(
        byte_kernel,
        out_shape=(
            out,
            out,
            jax.ShapeDtypeStruct(wgv.shape, f32),
            jax.ShapeDtypeStruct(wgo.shape, f32),
        ),
        in_specs=[hbm] * 8,
        out_specs=[hbm] * 4,
        scratch_shapes=[
            pltpu.SMEM(tab.shape, jnp.int32), pltpu.VMEM(table.shape, f32),
            pltpu.VMEM(means.shape, f32), pltpu.VMEM(bd.shape, bf), pltpu.VMEM(expo.shape, bf), pltpu.VMEM(pgrad.shape, bf),
            pltpu.VMEM(out.shape, bf), pltpu.VMEM(out.shape, bf),
            pltpu.VMEM((2,) + wgv.shape, f32),
            dma((ngroup,)), dma((ngroup,)), dma((nchunk,)), dma((nchunk,)), dma((4,)), dma((4,)),
        ],
        compiler_params=pltpu.CompilerParams(vmem_limit_bytes=60 * 1024 * 1024),
    )(tab, table, means, bd, expo, pgrad, wgv, wgo)


def on_device_kernels(
    ndp, nt, patch_states, residual_grad, upstream_value, norm_gain, value_weight, out_weight,
    attn_out, queries, byte_keys, byte_values, patch_starts,
):
    wgv, wgo, bd, expo, pgrad, tab, table, means = grad_call(
        ndp, nt, patch_states[0], residual_grad[0], upstream_value[0],
        norm_gain.reshape(-1, 128), value_weight, out_weight, attn_out[0], queries[0], patch_starts,
        byte_keys.reshape(-1, BLK, HD), byte_values.reshape(-1, BLK, HD),
    )
    gk, gv, wgv, wgo = byte_call(
        tab, table, means, bd, expo, pgrad, wgv, wgo.reshape(wgv.shape),
        jax.ShapeDtypeStruct(byte_keys[0].shape, jnp.bfloat16),
    )
    return (wgv, wgo, gk[None], gv[None])


def solution(mesh):
    ndp, nseq, nt = mesh.shape["dp"], mesh.shape["seq"], mesh.shape["tensor"]
    use_kernels = nseq == 2 and ndp == 4
    body = functools.partial(on_device_kernels, ndp, nt) if use_kernels else on_device
    return jax.shard_map(
        body,
        mesh=mesh,
        in_specs=(
            P("dp", "seq", "tensor"),
            P("dp", "seq", "tensor"),
            P("dp", "seq", None),
            P("tensor"),
            P(("dp", "seq"), "tensor"),
            P(("dp", "seq"), "tensor"),
            P("dp", "seq", None),
            P("dp", "seq", "tensor"),
            P("dp", "seq", "tensor"),
            P("dp", "seq", "tensor"),
            P("dp", None),
        ),
        out_specs=(
            P(("dp", "seq"), "tensor"),
            P(("dp", "seq"), "tensor"),
            P("dp", "seq", "tensor"),
            P("dp", "seq", "tensor"),
        ),
        check_vma=False,
    )
```

```python
import functools
import math

import jax
import jax.numpy as jnp
from jax import lax
from jax.experimental import pallas as pl
from jax.experimental.pallas import tpu as pltpu
from jax.sharding import PartitionSpec as P

HD = 128


def member_sum(member32, terms):
    return lax.dot_general(
        member32,
        terms,
        (((0,), (0,)), ((), ())),
        precision=lax.Precision.HIGHEST,
        preferred_element_type=jnp.float32,
    )


def member_spread(member32, totals):
    return jnp.dot(
        member32, totals, precision=lax.Precision.HIGHEST, preferred_element_type=jnp.float32
    )


def cross_backward(member, segment_rows, keys, values, head_width):
    nbytes = keys.shape[0]
    heads = keys.shape[1] // HD
    scale = 1.0 / math.sqrt(HD)
    member32 = member.astype(jnp.float32)
    picked = jnp.dot(member, segment_rows, preferred_element_type=jnp.float32).astype(jnp.bfloat16)
    grad_f = picked[:, :head_width].astype(jnp.float32).reshape(nbytes, heads, HD)
    query_f = picked[:, head_width:].astype(jnp.float32).reshape(nbytes, heads, HD)
    keys_f = keys.astype(jnp.float32).reshape(nbytes, heads, HD)
    values_f = values.astype(jnp.float32).reshape(nbytes, heads, HD)
    scores = jnp.sum(query_f * keys_f, axis=-1) * scale
    expo = jnp.exp(scores)
    totals = member_spread(member32, member_sum(member32, expo))
    probs = expo / totals
    grad_values = (probs[..., None] * grad_f).reshape(nbytes, heads * HD).astype(jnp.bfloat16)
    prob_grad = jnp.sum(grad_f * values_f, axis=-1)
    mass = member_spread(member32, member_sum(member32, probs * prob_grad))
    score_grad = probs * (prob_grad - mass)
    grad_keys = (
        (score_grad[..., None] * query_f * scale).reshape(nbytes, heads * HD).astype(jnp.bfloat16)
    )
    return (grad_keys, grad_values)


def contract_rows(left, right):
    return lax.dot_general(
        left, right, (((0,), (0,)), ((), ())), preferred_element_type=jnp.float32
    )


def on_device(
    patch_states,
    residual_grad,
    upstream_value,
    norm_gain,
    value_weight,
    out_weight,
    attn_out,
    queries,
    byte_keys,
    byte_values,
    patch_starts,
):
    states = patch_states[0]
    patches = states.shape[0]
    width_local = states.shape[1]
    model_width = width_local * lax.axis_size("tensor")
    states32 = states.astype(jnp.float32)
    gain32 = norm_gain.astype(jnp.float32)
    upstream = upstream_value[0]
    context = attn_out[0]
    value_full, out_full = (
        lax.all_gather(value_weight, ("dp", "seq"), axis=0, tiled=True),
        lax.all_gather(out_weight, ("dp", "seq"), axis=0, tiled=True),
    )
    grad_normed = jnp.dot(upstream, value_full, preferred_element_type=jnp.float32)
    square_part = jnp.sum(states32 * states32, axis=1)
    cross_part = jnp.sum(grad_normed * gain32 * states32, axis=1)
    square_sum, cross_sum = lax.psum((square_part, cross_part), "tensor")
    inv_rms = lax.rsqrt(square_sum / model_width + 1e-05)
    normed = (states32 * inv_rms[:, None] * gain32).astype(jnp.bfloat16)
    grad_patch = (
        residual_grad[0].astype(jnp.float32)
        + inv_rms[:, None] * gain32 * grad_normed
        - (inv_rms**3)[:, None] * states32 * (cross_sum / model_width)[:, None]
    ).astype(jnp.bfloat16)
    partial_attn = lax.dot_general(
        grad_patch, out_full, (((1,), (1,)), ((), ())), preferred_element_type=jnp.float32
    )
    columns = upstream
    wgrad_value = lax.psum_scatter(
        contract_rows(columns, normed), ("dp", "seq"), scatter_dimension=0, tiled=True
    )
    columns = context
    wgrad_out = lax.psum_scatter(
        contract_rows(columns, grad_patch), ("dp", "seq"), scatter_dimension=0, tiled=True
    )
    attn_all = lax.psum(partial_attn, "tensor").astype(jnp.bfloat16)
    head_width = queries.shape[2]
    grad_attn = lax.dynamic_slice_in_dim(
        attn_all, lax.axis_index("tensor") * head_width, head_width, 1
    )
    starts = patch_starts[0]
    total_patches = starts.shape[0]
    seq_count = lax.axis_size("seq")
    seq_pos = lax.axis_index("seq")
    byte_count = byte_keys.shape[1]
    window_len = 2 * patches
    owners = starts // byte_count
    shard_ids = jnp.arange(seq_count, dtype=jnp.int32)
    firsts = jnp.sum((owners[None, :] < shard_ids[:, None]).astype(jnp.int32), axis=1)
    my_first = jnp.sum(firsts * (shard_ids == seq_pos).astype(jnp.int32))
    payload = jnp.concatenate([grad_attn, queries[0]], axis=1)
    padded_starts = jnp.concatenate(
        [starts, jnp.full((window_len,), 2 * total_patches * byte_count + byte_count, jnp.int32)]
    )
    local_starts = lax.dynamic_slice_in_dim(padded_starts, my_first, window_len)
    positions = seq_pos * byte_count + jnp.arange(byte_count, dtype=jnp.int32)
    reached = local_starts[None, :] <= positions[:, None]
    after = jnp.concatenate([reached[:, 1:], jnp.zeros((byte_count, 1), bool)], axis=1)
    member = (reached & jnp.logical_not(after)).astype(jnp.bfloat16)
    mine = seq_pos * patches + jnp.arange(patches, dtype=jnp.int32)
    targets = lax.dynamic_slice_in_dim(owners, seq_pos * patches, patches)
    target_first = jnp.sum((owners[None, :] < targets[:, None]).astype(jnp.int32), axis=1)
    slots = mine - jnp.maximum(seq_pos * patches, target_first)
    dest = targets * patches + slots
    place = (jnp.arange(seq_count * patches, dtype=jnp.int32)[:, None] == dest[None, :]).astype(
        jnp.bfloat16
    )
    outgoing = jnp.dot(place, payload, preferred_element_type=jnp.float32).astype(jnp.bfloat16)
    outgoing = outgoing.reshape(seq_count, patches, 2 * head_width)
    incoming = lax.all_to_all(outgoing, "seq", split_axis=0, concat_axis=0, tiled=True)
    wanted = my_first + jnp.arange(window_len, dtype=jnp.int32)
    sources = wanted // patches
    received_row = sources * patches + wanted - jnp.maximum(sources * patches, my_first)
    select = (
        received_row[:, None] == jnp.arange(seq_count * patches, dtype=jnp.int32)[None, :]
    ).astype(jnp.bfloat16)
    segment_rows = jnp.dot(
        select,
        incoming.reshape(seq_count * patches, 2 * head_width),
        preferred_element_type=jnp.float32,
    ).astype(jnp.bfloat16)
    grad_keys, grad_values = cross_backward(
        member, segment_rows, byte_keys[0], byte_values[0], head_width
    )
    return (wgrad_value, wgrad_out, grad_keys[None], grad_values[None])


BLK = 256
GROUP = 8
WIN = 128


def tile_scores(b, w, keys, qb, bounds):
    s = lax.dot_general(keys[b], qb[w], (((1,), (1,)), ((), ())), preferred_element_type=jnp.float32)
    row = lax.broadcasted_iota(jnp.int32, (BLK, WIN), 0) + b * BLK
    limits = bounds[w]
    inside = (row >= limits[0:1, :]) & (row < limits[1:2, :])
    return jnp.where(inside, jnp.exp(s * (1.0 / math.sqrt(HD))), 0.0)


def tile_products(b, w, values, gb):
    return lax.dot_general(
        values[b], gb[w], (((1,), (1,)), ((), ())), preferred_element_type=jnp.float32
    )


def grad_kernel(
    ndp, nt, nbytes, states_in, resid_in, up_in, gain_in, vw, ow, ctx_in, q_in, starts,
    keys_in, values_in, wgv, wgo, bd_out, e_out, p_out, tab, table, means,
    states, resid, up, ctx, gain, wall, sqs, sqr, part, acc, acco, accz, rbz, lbz, ysz, yrz, rbv, lbv, ysv, yrv, rbo, lbo, yso, yro,
    pas, par, gn, nrm, gpat, trans_v, trans_o, gsend, gboth, qboth, keys, values, bd, qb, gb, bounds, expo, pgrad, psums, tab_s,
    s_in, s_e, s_p, s_out, s_ag, r_ag, s_sq, r_sq, s_rv, r_rv, s_lv, r_lv, s_ro, r_ro, s_lo, r_lo,
    s_rz, r_rz, s_lz, r_lz, s_yo, r_yo, s_yv, r_yv, s_pa, r_pa, s_g, r_g,
):
    dp, sq, tn = lax.axis_index("dp"), lax.axis_index("seq"), lax.axis_index("tensor")
    patches, width = states.shape
    model = width * nt
    last = ndp - 1
    mine = dp * 2 + sq
    tall = 128
    nrow = patches // tall
    ncol = width // 256

    right, left = (dp + 1, sq, tn), (dp - 1, sq, tn)
    ydev = (dp, 1 - sq, tn)

    def tdev(k):
        return (dp, sq, lax.rem(tn + k, nt))

    def copy(src, dst, ssem, rsem, dev):
        return pltpu.make_async_remote_copy(
            src_ref=src, dst_ref=dst, send_sem=ssem, recv_sem=rsem,
            device_id=dev, device_id_type=pl.DeviceIdType.MESH,
        )

    local = {}
    for i, (name, src, dst) in enumerate(
        (("states", states_in, states), ("up", up_in, up), ("resid", resid_in, resid),
         ("ctx", ctx_in, ctx), ("q", q_in, qboth.at[sq]), ("vw", vw, wall.at[0, mine]),
         ("ow", ow, wall.at[1, mine]), ("keys", keys_in, keys), ("values", values_in, values))
    ):
        local[name] = pltpu.make_async_copy(src, dst, s_in.at[i])
        local[name].start()

    barrier = pltpu.get_barrier_semaphore()
    peers = [(lax.rem(dp + k, ndp), sq, tn) for k in range(1, ndp)]
    peers += [tdev(k) for k in range(1, nt)] + [ydev]
    for dev in peers:
        pl.semaphore_signal(barrier, inc=1, device_id=dev, device_id_type=pl.DeviceIdType.MESH)
    pl.semaphore_wait(barrier, len(peers))

    sent = []

    def go(c, cond=None):
        if cond is None:
            c.start()
        else:
            pl.when(cond)(c.start)
        sent.append((c, cond))
        return c

    weights = (vw, ow)

    def half(h):
        return pl.ds(h * (vw.shape[0] // 2), vw.shape[0] // 2)

    def shard(w, zz, yy, h, dev, k, own=False):
        slot = zz * 2 + yy
        block = wall.at[w, slot, half(h)]
        src = weights[w].at[half(h)] if own else block
        return copy(src, block, s_ag.at[w, h, k], r_ag.at[w, h, slot], dev)

    def ag_own_z(w, h, ends=True, inner=True):
        for dev, onward, edge, k in ((right, dp < last, dp == 0, 0), (left, dp > 0, dp == last, 1)):
            if ends:
                go(shard(w, dp, sq, h, dev, k, True), edge)
            if inner:
                go(shard(w, dp, sq, h, dev, k, True), onward & jnp.logical_not(edge))

    def ag_own_y(w, h):
        go(shard(w, dp, sq, h, ydev, 2, True))

    def ag_forward(w, s, h):
        for zz, here, dev, onward, k in (
            (dp - s, dp - s >= 0, right, dp < last, 3 * s),
            (dp + s, dp + s <= last, left, dp > 0, 3 * ndp + 3 * s),
        ):
            pl.when(here)(shard(w, zz, sq, h, dev, k).wait_recv)
            go(shard(w, zz, sq, h, dev, k), here & onward)
            spread = here if w == 0 or s > 1 else here & ((zz == 0) | (zz == last))
            go(shard(w, zz, sq, h, ydev, k + 1), spread)

    def ag_cross(w, h):
        inner = (dp > 0) & (dp < last)
        pl.when(inner)(shard(w, dp, 1 - sq, h, ydev, 2).wait_recv)
        go(shard(w, dp, 1 - sq, h, right, 11), inner)
        go(shard(w, dp, 1 - sq, h, left, 12), inner)

    def ag_wait_y(w):
        for zz in range(ndp):
            for h in range(2):
                wait = shard(w, zz, 1 - sq, h, ydev, 2).wait_recv
                if w == 0 or zz in (0, last):
                    wait()
                else:
                    pl.when(dp != zz)(wait)

    def row_loop(fn):
        def body(i, _):
            fn(pl.ds(pl.multiple_of(i * tall, tall), tall), i)
            return 0

        lax.fori_loop(0, nrow, body, 0)

    def to_row(col):
        return jnp.broadcast_to(col, (tall, 128)).T[:8]

    def share(which):
        return [
            go(copy(sqs.at[which], sqr.at[which, k - 1], s_sq.at[which, k - 1],
                    r_sq.at[which, k - 1], tdev(k)))
            for k in range(1, nt)
        ]

    def total_col(which, i):
        rows = sqs[which, i]
        for k in range(nt - 1):
            rows = rows + sqr[which, k, i]
        return jnp.broadcast_to(rows[0:1, :], (128, tall)).T[:, 0:1]

    def inverse(i):
        return lax.rsqrt(total_col(0, i) / model + 1e-05)

    def square(here, i):
        x = states[here, :].astype(jnp.float32)
        sqs[0, i] = to_row(jnp.sum(x * x, axis=1, keepdims=True))

    def normalise(here, i):
        x = states[here, :].astype(jnp.float32)
        nrm[here, :] = (x * inverse(i) * gain[0:1, :]).astype(jnp.bfloat16)

    def wgrad(w, trans, factor):
        nblk, rows_per = part.shape[1], part.shape[2]

        def body(c, _):
            cols = pl.ds(pl.multiple_of(c * 256, 256), 256)
            out = jnp.dot(trans[...], factor[:, cols], preferred_element_type=jnp.float32)
            part[w, :, :, cols] = out.reshape(nblk, rows_per, 256)
            return 0

        lax.fori_loop(0, ncol, body, 0)

    def part_v(zz, h):
        return part[0, zz * 2 + h]

    def part_z(zz, h):
        return part[1, zz * 2 + h, half(1)]

    def part_o(zz, h):
        yo(zz, h).wait_recv()
        return part[1, zz * 2 + sq, half(h)] + yro[zz, h].astype(jnp.float32)

    def hops(d, h, buf_r, buf_l, s_r, r_r, s_l, r_l):
        for zz, valid, dev, fed, buf, ss, rs in (
            (dp + d, dp + d <= last, right, dp > 0, buf_r, s_r, r_r),
            (dp - d, dp - d >= 0, left, dp < last, buf_l, s_l, r_l),
        ):
            c = copy(buf.at[zz, h], buf.at[zz, h], ss.at[d - 1, h], rs.at[zz, h], dev)
            yield zz, valid, fed, buf, c

    def line_open(get, bufs, halves=(0, 1)):
        for d in range(last, 0, -1):
            for h in halves:
                for zz, valid, fed, buf, c in hops(d, h, *bufs):
                    opening = valid & jnp.logical_not(fed)

                    @pl.when(opening)
                    def _(zz=zz, h=h, buf=buf):
                        buf[zz, h] = get(zz, h).astype(jnp.bfloat16)

                    go(c, opening)

    def line(d, h, get, bufs):
        for zz, valid, fed, buf, c in hops(d, h, *bufs):

            @pl.when(valid & fed)
            def _(zz=zz, buf=buf, c=c):
                mine_part = get(zz, h)
                c.wait_recv()
                buf[zz, h] = (mine_part + buf[zz, h].astype(jnp.float32)).astype(jnp.bfloat16)

            go(c, valid & fed)

    def line_end(h, acc, bufs):
        buf_r, buf_l, s_r, r_r, s_l, r_l = bufs
        for fed, dev, buf, ss, rs in (
            (dp > 0, right, buf_r, s_r, r_r),
            (dp < last, left, buf_l, s_l, r_l),
        ):
            c = copy(buf.at[dp, h], buf.at[dp, h], ss.at[0, h], rs.at[dp, h], dev)

            @pl.when(fed)
            def _(c=c, buf=buf):
                c.wait_recv()
                acc[h] += buf[dp, h].astype(jnp.float32)

    line_v = (rbv, lbv, s_rv, r_rv, s_lv, r_lv)
    line_o = (rbo, lbo, s_ro, r_ro, s_lo, r_lo)
    line_z = (rbz, lbz, s_rz, r_rz, s_lz, r_lz)

    def yo(zz, h):
        return copy(yso.at[zz, h], yro.at[zz, h], s_yo.at[zz, h], r_yo.at[zz, h], ydev)

    def send_yo(zz, h, cond=None):
        def fill():
            yso[zz, h] = part[1, zz * 2 + (1 - sq), half(h)].astype(jnp.bfloat16)

        fill() if cond is None else pl.when(cond)(fill)
        go(yo(zz, h), cond)

    for h in range(2):
        ag_own_z(0, h)
        ag_own_y(0, h)
    for i in range(width // 128):
        gain[:, i * 128 : (i + 1) * 128] = jnp.broadcast_to(
            gain_in[i : i + 1, :].astype(jnp.float32), (8, 128)
        )
    local["states"].wait()
    row_loop(square)
    sq_copies = share(0)
    local["up"].wait()
    trans_v[...] = up[...].T

    first = starts[0:1, :] - sq * nbytes
    row8 = jnp.broadcast_to(first, (8, first.shape[1]))
    lane = lax.broadcasted_iota(jnp.int32, row8.shape, 1)
    after = jnp.where(
        lane == first.shape[1] - 1, 2 * nbytes, pltpu.roll(row8, first.shape[1] - 1, 1)
    )
    for w in range(first.shape[1] // WIN):
        lanes = slice(w * WIN, (w + 1) * WIN)
        bounds[w, 0:1, :] = first[:, lanes]
        bounds[w, 1:2, :] = after[0:1, lanes]
    bounds[first.shape[1] // WIN] = jnp.full(bounds.shape[1:], 4 * nbytes, jnp.int32)

    ag_forward(0, 1, 0)
    for h in range(2):
        ag_own_z(1, h, inner=False)
    for c in sq_copies:
        c.wait_recv()
    row_loop(normalise)
    ag_forward(0, 1, 1)
    wgrad(0, trans_v, nrm)
    line_open(part_v, line_v)
    ag_forward(0, 2, 0)
    nblocks = nbytes // BLK
    ends = lax.broadcasted_iota(jnp.int32, (nblocks, first.shape[1]), 0) * BLK + (BLK - 1)
    reach = (jnp.broadcast_to(first, ends.shape) <= ends).astype(jnp.int32)
    high = (jnp.sum(reach, axis=1, keepdims=True) - 1) // WIN
    low = (jnp.sum((first <= 0).astype(jnp.int32), axis=1, keepdims=True) - 1) // WIN
    step = lax.broadcasted_iota(jnp.int32, (nblocks, 128), 0) + high - low
    pair = lax.broadcasted_iota(jnp.int32, (nblocks, 128), 1)
    block_of = jnp.sum((step < pair).astype(jnp.int32), axis=0, keepdims=True)
    window = lax.broadcasted_iota(jnp.int32, (1, 128), 1) - block_of + low
    done = block_of >= nblocks
    tab[0:1, :] = jnp.where(done, nblocks - 1, block_of)
    nwin = first.shape[1] // WIN
    window = jnp.where(done, nwin, window)
    tab[1:2, :] = window
    window_of = jnp.broadcast_to(window.astype(jnp.float32), (128, 128)).T[: psums.shape[1], 0:1]
    local["tab"] = pltpu.make_async_copy(tab, tab_s, s_in.at[9])
    local["tab"].start()
    for w in range(nwin):
        bd[w, :WIN, HD:] = jnp.zeros((WIN, HD), jnp.bfloat16)
        bd[w, WIN:, :HD] = jnp.zeros((WIN, HD), jnp.bfloat16)
    bd[nwin] = jnp.zeros(bd.shape[1:], jnp.bfloat16)
    qb[nwin] = jnp.zeros((WIN, HD), jnp.bfloat16)
    gb[nwin] = jnp.zeros((WIN, HD), jnp.bfloat16)

    ag_forward(0, 2, 1)
    local["ctx"].wait()
    trans_o[...] = ctx[...].T
    for h in range(2):
        ag_forward(0, 3, h)
        ag_own_z(1, h, ends=False)
        ag_own_y(1, h)
    line(2, 0, part_v, line_v)
    ag_forward(1, 1, 0)
    local["vw"].wait()
    ag_wait_y(0)
    ag_forward(1, 1, 1)

    def project(here, i):
        full = wall[0].reshape(up.shape[1], width)
        g = jnp.dot(up[here, :], full, preferred_element_type=jnp.float32)
        gn[here, :] = g
        x = states[here, :].astype(jnp.float32)
        sqs[1, i] = to_row(jnp.sum(g * gain[0:1, :] * x, axis=1, keepdims=True))

    row_loop(project)
    cr_copies = share(1)
    line(2, 1, part_v, line_v)
    ag_cross(1, 0)
    ag_forward(1, 2, 0)
    ag_cross(1, 1)
    ag_forward(1, 2, 1)
    local["resid"].wait()
    for c in cr_copies:
        c.wait_recv()

    def make_grad(here, i):
        inv = inverse(i)
        cross = total_col(1, i) / model
        x = states[here, :].astype(jnp.float32)
        gpat[here, :] = (
            resid[here, :].astype(jnp.float32)
            + inv * gain[0:1, :] * gn[here, :]
            - (inv * inv * inv * cross) * x
        ).astype(jnp.bfloat16)

    row_loop(make_grad)
    ag_forward(1, 3, 0)
    ag_forward(1, 3, 1)
    local["q"].wait()
    qc = go(copy(qboth.at[sq], qboth.at[sq], s_g.at[0], r_g.at[0], ydev))
    wgrad(1, trans_o, gpat)
    line_open(part_z, line_z)
    for k in range(ndp - 1, 0, -1):
        send_yo(dp + k, 0, dp + k <= last)
        send_yo(dp - k, 0, dp - k >= 0)
    send_yo(dp, 0)
    for h in range(2):
        line(1, h, part_v, line_v)
    for h in range(2):
        line(2, h, part_z, line_z)
    local["ow"].wait()
    ag_wait_y(1)

    def tile(i):
        return pl.ds(i * tall, tall)

    def pa(i, k):
        return copy(gsend.at[k - 1, tile(i)], par.at[k - 1, tile(i)], s_pa.at[k - 1, i],
                    r_pa.at[k - 1, i], tdev(k))

    for i in range(nrow):
        full = wall[1].reshape(up.shape[1], width)
        p = lax.dot_general(
            gpat[tile(i), :], full, (((1,), (1,)), ((), ())), preferred_element_type=jnp.float32
        )
        for j in range(nt):
            pas[j, tile(i), :] = p[:, j * HD : (j + 1) * HD]
        for k in range(1, nt):
            gsend[k - 1, tile(i)] = pas[lax.rem(tn + k, nt), tile(i)].astype(jnp.bfloat16)
            go(pa(i, k))

    for h in range(2):
        acc[h] = part_v(dp, h)
        line_end(h, acc, line_v)
    ysv[...] = acc[1 - sq].astype(jnp.bfloat16)
    yv = go(copy(ysv, yrv, s_yv.at[0], r_yv.at[0], ydev))
    ngroup = psums.shape[1] // GROUP

    def e_copy(group):
        here = pl.ds(group * GROUP, GROUP)
        return pltpu.make_async_copy(expo.at[here], e_out.at[here], s_e.at[group])

    def p_copy(group):
        here = pl.ds(group * GROUP, GROUP)
        return pltpu.make_async_copy(pgrad.at[here], p_out.at[here], s_p.at[group])

    def scores(group, _):
        for k in range(GROUP):
            n = group * GROUP + k
            e = tile_scores(tab_s[0, n], tab_s[1, n], keys, qb, bounds).astype(jnp.bfloat16)
            expo[n] = e
            psums[0, pl.ds(n, 1), :] = jnp.sum(e.astype(jnp.float32), axis=0, keepdims=True)
        e_copy(group).start()
        return 0

    def products(group, _):
        for k in range(GROUP):
            n = group * GROUP + k
            pg = tile_products(tab_s[0, n], tab_s[1, n], values, gb)
            t = psums[0, pl.ds(n, 1), :]
            m = jnp.sum(expo[n].astype(jnp.float32) * pg, axis=0, keepdims=True)
            mean = m / jnp.where(t > 0.0, t, 1.0)
            pgrad[n] = (pg - mean).astype(jnp.bfloat16)
            psums[1, pl.ds(n, 1), :] = m
            means[pl.ds(n, 1), :] = mean
        p_copy(group).start()
        return 0

    def window_rows(w):
        return (w * WIN // patches, pl.ds(w * WIN % patches, WIN))

    def window_total(which, w):
        return jnp.sum(
            jnp.where(window_of == float(w), psums[which], 0.0), axis=0, keepdims=True
        )

    def open_scores():
        qc.wait_recv()
        for name in ("keys", "values", "tab"):
            local[name].wait()
        for w in range(nwin):
            rows = qboth[window_rows(w)]
            qb[w] = rows
            bd[w, :WIN, :HD] = rows

    def close_scores():
        for w in range(nwin):
            t = window_total(0, w)
            table[0:1, w * WIN : (w + 1) * WIN] = jnp.where(
                t > 0.0, 1.0 / jnp.where(t > 0.0, t, 1.0), 0.0
            )
        table[:, nwin * WIN :] = jnp.zeros((2, WIN), jnp.float32)

    open_scores()
    lax.fori_loop(0, ngroup, scores, 0)
    close_scores()
    line_open(part_o, line_o, (0,))
    for h in range(2):
        line(1, h, part_z, line_z)
    line(2, 0, part_o, line_o)
    gc = []
    for i in range(nrow):
        total = pas[tn, tile(i)]
        for k in range(1, nt):
            pa(i, k).wait_recv()
            total = total + par[k - 1, tile(i)].astype(jnp.float32)
        gboth[sq, tile(i)] = total.astype(jnp.bfloat16)
        block = gboth.at[sq, tile(i)]
        gc.append(go(copy(block, block, s_g.at[1 + i], r_g.at[1 + i], ydev)))
    for h in range(2):
        accz[h] = part_z(dp, h)
        line_end(h, accz, line_z)
    ysz[...] = accz[1 - sq].astype(jnp.bfloat16)
    yz = go(copy(ysz, yrz, s_yv.at[1], r_yv.at[1], ydev))
    line(1, 0, part_o, line_o)
    yv.wait_recv()
    acc[0] = acc[sq] + yrv[...].astype(jnp.float32)
    out_v = pltpu.make_async_copy(acc.at[0], wgv, s_out.at[0])
    out_v.start()
    for c in gc:
        c.wait_recv()
    for w in range(nwin):
        rows = gboth[window_rows(w)]
        gb[w] = rows
        bd[w, WIN:, HD:] = rows
    out_bd = pltpu.make_async_copy(bd, bd_out, s_out.at[2])
    out_bd.start()
    lax.fori_loop(0, ngroup, products, 0)
    for w in range(nwin):
        lanes = slice(w * WIN, (w + 1) * WIN)
        table[1:2, lanes] = window_total(1, w) * table[0:1, lanes]
    acco[0] = part_o(dp, 0)
    line_end(0, acco, line_o)
    yz.wait_recv()
    acco[1] = accz[sq] + yrz[...].astype(jnp.float32)
    out_o = pltpu.make_async_copy(acco, wgo, s_out.at[1])
    out_o.start()
    for group in range(ngroup):
        e_copy(group).wait()
        p_copy(group).wait()
    for c, cond in sent:
        if cond is None:
            c.wait_send()
        else:
            pl.when(cond)(c.wait_send)
    for c in (out_v, out_o, out_bd):
        c.wait()


def grad_call(ndp, nt, states, resid, up, gain, vw, ow, ctx, q, starts, keys, values):
    patches, width = states.shape
    rows = vw.shape[0]
    nblk = 2 * ndp
    nk = up.shape[1]
    bf, f32, i32 = jnp.bfloat16, jnp.float32, jnp.int32
    nrow = patches // 128
    nbytes = keys.shape[0] * BLK
    total = starts.shape[1]
    nwin = total // WIN
    npair = -(-(nbytes // BLK + nwin - 1) // GROUP) * GROUP
    vmem = pl.BlockSpec(memory_space=pltpu.VMEM)
    hbm = pl.BlockSpec(memory_space=pl.ANY)
    dma = pltpu.SemaphoreType.DMA
    return pl.pallas_call(
        functools.partial(grad_kernel, ndp, nt, nbytes),
        out_shape=(
            jax.ShapeDtypeStruct((rows, width), f32),
            jax.ShapeDtypeStruct((2, rows // 2, width), f32),
            jax.ShapeDtypeStruct((nwin + 1, 2 * WIN, 2 * HD), bf),
            jax.ShapeDtypeStruct((npair, BLK, WIN), bf),
            jax.ShapeDtypeStruct((npair, BLK, WIN), bf),
            jax.ShapeDtypeStruct((2, 128), i32),
            jax.ShapeDtypeStruct((2, total + WIN), f32),
            jax.ShapeDtypeStruct((npair, WIN), f32),
        ),
        in_specs=[hbm, hbm, hbm, vmem, hbm, hbm, hbm, hbm, vmem, hbm, hbm],
        out_specs=[hbm] * 5 + [vmem] * 3,
        scratch_shapes=[
            pltpu.VMEM((patches, width), bf),
            pltpu.VMEM((patches, width), bf),
            pltpu.VMEM((patches, nk), bf),
            pltpu.VMEM((patches, nk), bf),
            pltpu.VMEM((8, width), f32),
            pltpu.VMEM((2, nblk, rows, width), bf),
            pltpu.VMEM((2, nrow, 8, 128), f32),
            pltpu.VMEM((2, nt - 1, nrow, 8, 128), f32),
            pltpu.VMEM((2, nblk, rows, width), f32),
            pltpu.VMEM((2, rows, width), f32),
            pltpu.VMEM((2, rows // 2, width), f32),
            pltpu.VMEM((2, rows // 2, width), f32),
            pltpu.VMEM((ndp, 2, rows // 2, width), bf),
            pltpu.VMEM((ndp, 2, rows // 2, width), bf),
            pltpu.VMEM((rows // 2, width), bf),
            pltpu.VMEM((rows // 2, width), bf),
            pltpu.VMEM((ndp, 2, rows, width), bf),
            pltpu.VMEM((ndp, 2, rows, width), bf),
            pltpu.VMEM((rows, width), bf),
            pltpu.VMEM((rows, width), bf),
            pltpu.VMEM((ndp, 2, rows // 2, width), bf),
            pltpu.VMEM((ndp, 2, rows // 2, width), bf),
            pltpu.VMEM((ndp, 2, rows // 2, width), bf),
            pltpu.VMEM((ndp, 2, rows // 2, width), bf),
            pltpu.VMEM((nt, patches, HD), f32),
            pltpu.VMEM((nt - 1, patches, HD), bf),
            pltpu.VMEM((patches, width), f32),
            pltpu.VMEM((patches, width), bf),
            pltpu.VMEM((patches, width), bf),
            pltpu.VMEM((nk, patches), bf),
            pltpu.VMEM((nk, patches), bf),
            pltpu.VMEM((nt - 1, patches, HD), bf),
            pltpu.VMEM((2, patches, HD), bf),
            pltpu.VMEM((2, patches, HD), bf),
            pltpu.VMEM(keys.shape, bf),
            pltpu.VMEM(keys.shape, bf),
            pltpu.VMEM((nwin + 1, 2 * WIN, 2 * HD), bf),
            pltpu.VMEM((nwin + 1, WIN, HD), bf),
            pltpu.VMEM((nwin + 1, WIN, HD), bf),
            pltpu.VMEM((nwin + 1, 2, WIN), i32),
            pltpu.VMEM((npair, BLK, WIN), bf),
            pltpu.VMEM((npair, BLK, WIN), bf),
            pltpu.VMEM((2, npair, WIN), f32),
            pltpu.SMEM((2, 128), i32),
            dma((10,)), dma((npair // GROUP,)), dma((npair // GROUP,)), dma((3,)),
            dma((2, 2, 6 * ndp)), dma((2, 2, nblk)),
            dma((2, nt - 1)), dma((2, nt - 1)),
            dma((ndp, 2)), dma((ndp, 2)), dma((ndp, 2)), dma((ndp, 2)),
            dma((ndp, 2)), dma((ndp, 2)), dma((ndp, 2)), dma((ndp, 2)),
            dma((ndp, 2)), dma((ndp, 2)), dma((ndp, 2)), dma((ndp, 2)),
            dma((ndp, 2)), dma((ndp, 2)), dma((2,)), dma((2,)),
            dma((nt - 1, nrow)), dma((nt - 1, nrow)), dma((1 + nrow,)), dma((1 + nrow,)),
        ],
        compiler_params=pltpu.CompilerParams(
            collective_id=0, has_side_effects=True, vmem_limit_bytes=60 * 1024 * 1024
        ),
    )(states, resid, up, gain, vw, ow, ctx, q, starts, keys, values)


def byte_kernel(
    tab_in, table_in, means_in, bd_in, e_in, p_in, wgv_in, wgo_in, gk_out, gv_out, wgv, wgo,
    tab, table, means, bd, expo, pgrad, gk, gv, held, s_e, s_p, o_k, o_v, s_w, s_t,
):
    nwin = bd.shape[0] - 1
    nbytes = gk.shape[0]
    ngroup = expo.shape[0] // GROUP
    nchunk = o_k.shape[0]
    chunk = nbytes // nchunk
    ready = GROUP * BLK // chunk
    behind = -(-(nwin - 1) // (chunk // BLK))
    scale = 1.0 / math.sqrt(HD)

    def load(c):
        here = pl.ds(c * GROUP, GROUP)
        return (
            pltpu.make_async_copy(e_in.at[here], expo.at[here], s_e.at[c]),
            pltpu.make_async_copy(p_in.at[here], pgrad.at[here], s_p.at[c]),
        )

    def store(c):
        here = pl.ds(pl.multiple_of(c * chunk, chunk), chunk)
        return (
            pltpu.make_async_copy(gk.at[here], gk_out.at[here], o_k.at[c]),
            pltpu.make_async_copy(gv.at[here], gv_out.at[here], o_v.at[c]),
        )

    small = [
        pltpu.make_async_copy(a, b, s_t.at[i])
        for i, (a, b) in enumerate((
            (tab_in, tab), (table_in, table), (means_in, means), (bd_in, bd)
        ))
    ]
    for x in small:
        x.start()
    for c in range(ngroup):
        for x in load(c):
            x.start()
    carried = ((wgv_in, wgv), (wgo_in, wgo))
    taken = [pltpu.make_async_copy(a, held.at[i], s_w.at[i]) for i, (a, _) in enumerate(carried)]
    passed = [pltpu.make_async_copy(held.at[i], b, s_w.at[2 + i]) for i, (_, b) in enumerate(carried)]
    for x in taken:
        x.start()
    for x in small:
        x.wait()

    def apply(group, _):
        for x in load(group):
            x.wait()
        first = group * GROUP
        prior = jnp.maximum(first - 1, 0)
        before = pl.ds(pl.multiple_of(tab[0, prior] * BLK, BLK), BLK)
        held_k, held_v = gk[before, :], gv[before, :]
        for k in range(GROUP):
            n = first + k
            b, w = tab[0, n], tab[1, n]
            here = pl.ds(pl.multiple_of(b * BLK, BLK), BLK)
            lanes = pl.ds(pl.multiple_of(w * WIN, WIN), WIN)
            same = tab[0, jnp.maximum(n - 1, 0)] == b
            same = same & (n > 0) if k == 0 else same
            p = expo[n].astype(jnp.float32) * table[0:1, lanes]
            shift = means[pl.ds(n, 1), :] - table[1:2, lanes]
            sg = p * (pgrad[n].astype(jnp.float32) + shift) * scale
            both = jnp.concatenate([sg.astype(jnp.bfloat16), p.astype(jnp.bfloat16)], axis=1)
            out = jnp.dot(both, bd[w], preferred_element_type=jnp.float32).astype(jnp.bfloat16)
            held_k = out[:, :HD] + jnp.where(same, held_k, jnp.zeros_like(held_k))
            held_v = out[:, HD:] + jnp.where(same, held_v, jnp.zeros_like(held_v))
            gk[here, :] = held_k
            gv[here, :] = held_v

        for r in range(ready):
            done = group * ready + r - behind

            @pl.when((done >= 0) & (done < nchunk))
            def _(done=done):
                for x in store(done):
                    x.start()

        return 0

    lax.fori_loop(0, 1, apply, 0)
    for x, y in zip(taken, passed):
        x.wait()
        y.start()
    lax.fori_loop(1, ngroup, apply, 0)
    for c in range(max(ngroup * ready - behind, 0), nchunk):
        for x in store(c):
            x.start()
    for c in range(nchunk):
        for x in store(c):
            x.wait()
    for x in passed:
        x.wait()


def byte_call(tab, table, means, bd, expo, pgrad, wgv, wgo, out):
    bf, f32 = jnp.bfloat16, jnp.float32
    nchunk = out.shape[0] // 2048
    ngroup = expo.shape[0] // GROUP
    hbm = pl.BlockSpec(memory_space=pl.ANY)
    dma = pltpu.SemaphoreType.DMA
    return pl.pallas_call(
        byte_kernel,
        out_shape=(
            out,
            out,
            jax.ShapeDtypeStruct(wgv.shape, f32),
            jax.ShapeDtypeStruct(wgo.shape, f32),
        ),
        in_specs=[hbm] * 8,
        out_specs=[hbm] * 4,
        scratch_shapes=[
            pltpu.SMEM(tab.shape, jnp.int32), pltpu.VMEM(table.shape, f32),
            pltpu.VMEM(means.shape, f32), pltpu.VMEM(bd.shape, bf), pltpu.VMEM(expo.shape, bf), pltpu.VMEM(pgrad.shape, bf),
            pltpu.VMEM(out.shape, bf), pltpu.VMEM(out.shape, bf),
            pltpu.VMEM((2,) + wgv.shape, f32),
            dma((ngroup,)), dma((ngroup,)), dma((nchunk,)), dma((nchunk,)), dma((4,)), dma((4,)),
        ],
        compiler_params=pltpu.CompilerParams(vmem_limit_bytes=60 * 1024 * 1024),
    )(tab, table, means, bd, expo, pgrad, wgv, wgo)


def on_device_kernels(
    ndp, nt, patch_states, residual_grad, upstream_value, norm_gain, value_weight, out_weight,
    attn_out, queries, byte_keys, byte_values, patch_starts,
):
    wgv, wgo, bd, expo, pgrad, tab, table, means = grad_call(
        ndp, nt, patch_states[0], residual_grad[0], upstream_value[0],
        norm_gain.reshape(-1, 128), value_weight, out_weight, attn_out[0], queries[0], patch_starts,
        byte_keys.reshape(-1, BLK, HD), byte_values.reshape(-1, BLK, HD),
    )
    gk, gv, wgv, wgo = byte_call(
        tab, table, means, bd, expo, pgrad, wgv, wgo.reshape(wgv.shape),
        jax.ShapeDtypeStruct(byte_keys[0].shape, jnp.bfloat16),
    )
    return (wgv, wgo, gk[None], gv[None])


def solution(mesh):
    ndp, nseq, nt = mesh.shape["dp"], mesh.shape["seq"], mesh.shape["tensor"]
    use_kernels = nseq == 2 and ndp == 4
    body = functools.partial(on_device_kernels, ndp, nt) if use_kernels else on_device
    return jax.shard_map(
        body,
        mesh=mesh,
        in_specs=(
            P("dp", "seq", "tensor"),
            P("dp", "seq", "tensor"),
            P("dp", "seq", None),
            P("tensor"),
            P(("dp", "seq"), "tensor"),
            P(("dp", "seq"), "tensor"),
            P("dp", "seq", None),
            P("dp", "seq", "tensor"),
            P("dp", "seq", "tensor"),
            P("dp", "seq", "tensor"),
            P("dp", None),
        ),
        out_specs=(
            P(("dp", "seq"), "tensor"),
            P(("dp", "seq"), "tensor"),
            P("dp", "seq", "tensor"),
            P("dp", "seq", "tensor"),
        ),
        check_vma=False,
    )
```

```python
import functools
import math

import jax
import jax.numpy as jnp
from jax import lax
from jax.experimental import pallas as pl
from jax.experimental.pallas import tpu as pltpu
from jax.sharding import PartitionSpec as P

HD = 128


def member_sum(member32, terms):
    return lax.dot_general(
        member32,
        terms,
        (((0,), (0,)), ((), ())),
        precision=lax.Precision.HIGHEST,
        preferred_element_type=jnp.float32,
    )


def member_spread(member32, totals):
    return jnp.dot(
        member32, totals, precision=lax.Precision.HIGHEST, preferred_element_type=jnp.float32
    )


def cross_backward(member, segment_rows, keys, values, head_width):
    nbytes = keys.shape[0]
    heads = keys.shape[1] // HD
    scale = 1.0 / math.sqrt(HD)
    member32 = member.astype(jnp.float32)
    picked = jnp.dot(member, segment_rows, preferred_element_type=jnp.float32).astype(jnp.bfloat16)
    grad_f = picked[:, :head_width].astype(jnp.float32).reshape(nbytes, heads, HD)
    query_f = picked[:, head_width:].astype(jnp.float32).reshape(nbytes, heads, HD)
    keys_f = keys.astype(jnp.float32).reshape(nbytes, heads, HD)
    values_f = values.astype(jnp.float32).reshape(nbytes, heads, HD)
    scores = jnp.sum(query_f * keys_f, axis=-1) * scale
    expo = jnp.exp(scores)
    totals = member_spread(member32, member_sum(member32, expo))
    probs = expo / totals
    grad_values = (probs[..., None] * grad_f).reshape(nbytes, heads * HD).astype(jnp.bfloat16)
    prob_grad = jnp.sum(grad_f * values_f, axis=-1)
    mass = member_spread(member32, member_sum(member32, probs * prob_grad))
    score_grad = probs * (prob_grad - mass)
    grad_keys = (
        (score_grad[..., None] * query_f * scale).reshape(nbytes, heads * HD).astype(jnp.bfloat16)
    )
    return (grad_keys, grad_values)


def contract_rows(left, right):
    return lax.dot_general(
        left, right, (((0,), (0,)), ((), ())), preferred_element_type=jnp.float32
    )


def on_device(
    patch_states,
    residual_grad,
    upstream_value,
    norm_gain,
    value_weight,
    out_weight,
    attn_out,
    queries,
    byte_keys,
    byte_values,
    patch_starts,
):
    states = patch_states[0]
    patches = states.shape[0]
    width_local = states.shape[1]
    model_width = width_local * lax.axis_size("tensor")
    states32 = states.astype(jnp.float32)
    gain32 = norm_gain.astype(jnp.float32)
    upstream = upstream_value[0]
    context = attn_out[0]
    value_full, out_full = (
        lax.all_gather(value_weight, ("dp", "seq"), axis=0, tiled=True),
        lax.all_gather(out_weight, ("dp", "seq"), axis=0, tiled=True),
    )
    grad_normed = jnp.dot(upstream, value_full, preferred_element_type=jnp.float32)
    square_part = jnp.sum(states32 * states32, axis=1)
    cross_part = jnp.sum(grad_normed * gain32 * states32, axis=1)
    square_sum, cross_sum = lax.psum((square_part, cross_part), "tensor")
    inv_rms = lax.rsqrt(square_sum / model_width + 1e-05)
    normed = (states32 * inv_rms[:, None] * gain32).astype(jnp.bfloat16)
    grad_patch = (
        residual_grad[0].astype(jnp.float32)
        + inv_rms[:, None] * gain32 * grad_normed
        - (inv_rms**3)[:, None] * states32 * (cross_sum / model_width)[:, None]
    ).astype(jnp.bfloat16)
    partial_attn = lax.dot_general(
        grad_patch, out_full, (((1,), (1,)), ((), ())), preferred_element_type=jnp.float32
    )
    columns = upstream
    wgrad_value = lax.psum_scatter(
        contract_rows(columns, normed), ("dp", "seq"), scatter_dimension=0, tiled=True
    )
    columns = context
    wgrad_out = lax.psum_scatter(
        contract_rows(columns, grad_patch), ("dp", "seq"), scatter_dimension=0, tiled=True
    )
    attn_all = lax.psum(partial_attn, "tensor").astype(jnp.bfloat16)
    head_width = queries.shape[2]
    grad_attn = lax.dynamic_slice_in_dim(
        attn_all, lax.axis_index("tensor") * head_width, head_width, 1
    )
    starts = patch_starts[0]
    total_patches = starts.shape[0]
    seq_count = lax.axis_size("seq")
    seq_pos = lax.axis_index("seq")
    byte_count = byte_keys.shape[1]
    window_len = 2 * patches
    owners = starts // byte_count
    shard_ids = jnp.arange(seq_count, dtype=jnp.int32)
    firsts = jnp.sum((owners[None, :] < shard_ids[:, None]).astype(jnp.int32), axis=1)
    my_first = jnp.sum(firsts * (shard_ids == seq_pos).astype(jnp.int32))
    payload = jnp.concatenate([grad_attn, queries[0]], axis=1)
    padded_starts = jnp.concatenate(
        [starts, jnp.full((window_len,), 2 * total_patches * byte_count + byte_count, jnp.int32)]
    )
    local_starts = lax.dynamic_slice_in_dim(padded_starts, my_first, window_len)
    positions = seq_pos * byte_count + jnp.arange(byte_count, dtype=jnp.int32)
    reached = local_starts[None, :] <= positions[:, None]
    after = jnp.concatenate([reached[:, 1:], jnp.zeros((byte_count, 1), bool)], axis=1)
    member = (reached & jnp.logical_not(after)).astype(jnp.bfloat16)
    mine = seq_pos * patches + jnp.arange(patches, dtype=jnp.int32)
    targets = lax.dynamic_slice_in_dim(owners, seq_pos * patches, patches)
    target_first = jnp.sum((owners[None, :] < targets[:, None]).astype(jnp.int32), axis=1)
    slots = mine - jnp.maximum(seq_pos * patches, target_first)
    dest = targets * patches + slots
    place = (jnp.arange(seq_count * patches, dtype=jnp.int32)[:, None] == dest[None, :]).astype(
        jnp.bfloat16
    )
    outgoing = jnp.dot(place, payload, preferred_element_type=jnp.float32).astype(jnp.bfloat16)
    outgoing = outgoing.reshape(seq_count, patches, 2 * head_width)
    incoming = lax.all_to_all(outgoing, "seq", split_axis=0, concat_axis=0, tiled=True)
    wanted = my_first + jnp.arange(window_len, dtype=jnp.int32)
    sources = wanted // patches
    received_row = sources * patches + wanted - jnp.maximum(sources * patches, my_first)
    select = (
        received_row[:, None] == jnp.arange(seq_count * patches, dtype=jnp.int32)[None, :]
    ).astype(jnp.bfloat16)
    segment_rows = jnp.dot(
        select,
        incoming.reshape(seq_count * patches, 2 * head_width),
        preferred_element_type=jnp.float32,
    ).astype(jnp.bfloat16)
    grad_keys, grad_values = cross_backward(
        member, segment_rows, byte_keys[0], byte_values[0], head_width
    )
    return (wgrad_value, wgrad_out, grad_keys[None], grad_values[None])


BLK = 256
GROUP = 8
WIN = 128


def tile_scores(b, w, keys, qb, bounds):
    s = lax.dot_general(keys[b], qb[w], (((1,), (1,)), ((), ())), preferred_element_type=jnp.float32)
    row = lax.broadcasted_iota(jnp.int32, (BLK, WIN), 0) + b * BLK
    limits = bounds[w]
    inside = (row >= limits[0:1, :]) & (row < limits[1:2, :])
    return jnp.where(inside, jnp.exp(s * (1.0 / math.sqrt(HD))), 0.0)


def tile_products(b, w, values, gb):
    return lax.dot_general(
        values[b], gb[w], (((1,), (1,)), ((), ())), preferred_element_type=jnp.float32
    )


def grad_kernel(
    ndp, nt, nbytes, states_in, resid_in, up_in, gain_in, vw, ow, ctx_in, q_in, starts,
    keys_in, values_in, wgv, wgo, bd_out, e_out, p_out, tab, table, means,
    states, resid, up, ctx, gain, wall, sqs, sqr, part, acc, acco, accz, rbz, lbz, ysz, yrz, rbv, lbv, ysv, yrv, rbo, lbo, yso, yro,
    pas, par, gn, nrm, gpat, trans_v, trans_o, gsend, gboth, qboth, keys, values, bd, qb, gb, bounds, expo, pgrad, psums, tab_s,
    s_in, s_e, s_p, s_out, s_ag, r_ag, s_sq, r_sq, s_rv, r_rv, s_lv, r_lv, s_ro, r_ro, s_lo, r_lo,
    s_rz, r_rz, s_lz, r_lz, s_yo, r_yo, s_yv, r_yv, s_pa, r_pa, s_g, r_g,
):
    dp, sq, tn = lax.axis_index("dp"), lax.axis_index("seq"), lax.axis_index("tensor")
    patches, width = states.shape
    model = width * nt
    last = ndp - 1
    mine = dp * 2 + sq
    tall = 128
    nrow = patches // tall
    ncol = width // 256

    right, left = (dp + 1, sq, tn), (dp - 1, sq, tn)
    ydev = (dp, 1 - sq, tn)

    def tdev(k):
        return (dp, sq, lax.rem(tn + k, nt))

    def copy(src, dst, ssem, rsem, dev):
        return pltpu.make_async_remote_copy(
            src_ref=src, dst_ref=dst, send_sem=ssem, recv_sem=rsem,
            device_id=dev, device_id_type=pl.DeviceIdType.MESH,
        )

    local = {}
    for i, (name, src, dst) in enumerate(
        (("states", states_in, states), ("up", up_in, up), ("resid", resid_in, resid),
         ("ctx", ctx_in, ctx), ("q", q_in, qboth.at[sq]), ("vw", vw, wall.at[0, mine]),
         ("ow", ow, wall.at[1, mine]), ("keys", keys_in, keys), ("values", values_in, values))
    ):
        local[name] = pltpu.make_async_copy(src, dst, s_in.at[i])
        local[name].start()

    barrier = pltpu.get_barrier_semaphore()
    peers = [(lax.rem(dp + k, ndp), sq, tn) for k in range(1, ndp)]
    peers += [tdev(k) for k in range(1, nt)] + [ydev]
    for dev in peers:
        pl.semaphore_signal(barrier, inc=1, device_id=dev, device_id_type=pl.DeviceIdType.MESH)
    pl.semaphore_wait(barrier, len(peers))

    sent = []

    def go(c, cond=None):
        if cond is None:
            c.start()
        else:
            pl.when(cond)(c.start)
        sent.append((c, cond))
        return c

    weights = (vw, ow)

    def half(h):
        return pl.ds(h * (vw.shape[0] // 2), vw.shape[0] // 2)

    def shard(w, zz, yy, h, dev, k, own=False):
        slot = zz * 2 + yy
        block = wall.at[w, slot, half(h)]
        src = weights[w].at[half(h)] if own else block
        return copy(src, block, s_ag.at[w, h, k], r_ag.at[w, h, slot], dev)

    def ag_own_z(w, h, ends=True, inner=True):
        for dev, onward, edge, k in ((right, dp < last, dp == 0, 0), (left, dp > 0, dp == last, 1)):
            if ends:
                go(shard(w, dp, sq, h, dev, k, True), edge)
            if inner:
                go(shard(w, dp, sq, h, dev, k, True), onward & jnp.logical_not(edge))

    def ag_own_y(w, h):
        go(shard(w, dp, sq, h, ydev, 2, True))

    def ag_forward(w, s, h):
        for zz, here, dev, onward, k in (
            (dp - s, dp - s >= 0, right, dp < last, 3 * s),
            (dp + s, dp + s <= last, left, dp > 0, 3 * ndp + 3 * s),
        ):
            pl.when(here)(shard(w, zz, sq, h, dev, k).wait_recv)
            go(shard(w, zz, sq, h, dev, k), here & onward)
            spread = here if w == 0 or s > 1 else here & ((zz == 0) | (zz == last))
            go(shard(w, zz, sq, h, ydev, k + 1), spread)

    def ag_cross(w, h):
        inner = (dp > 0) & (dp < last)
        pl.when(inner)(shard(w, dp, 1 - sq, h, ydev, 2).wait_recv)
        go(shard(w, dp, 1 - sq, h, right, 11), inner)
        go(shard(w, dp, 1 - sq, h, left, 12), inner)

    def ag_wait_y(w):
        for zz in range(ndp):
            for h in range(2):
                wait = shard(w, zz, 1 - sq, h, ydev, 2).wait_recv
                if w == 0 or zz in (0, last):
                    wait()
                else:
                    pl.when(dp != zz)(wait)

    def row_loop(fn):
        def body(i, _):
            fn(pl.ds(pl.multiple_of(i * tall, tall), tall), i)
            return 0

        lax.fori_loop(0, nrow, body, 0)

    def to_row(col):
        return jnp.broadcast_to(col, (tall, 128)).T[:8]

    def share(which):
        return [
            go(copy(sqs.at[which], sqr.at[which, k - 1], s_sq.at[which, k - 1],
                    r_sq.at[which, k - 1], tdev(k)))
            for k in range(1, nt)
        ]

    def total_col(which, i):
        rows = sqs[which, i]
        for k in range(nt - 1):
            rows = rows + sqr[which, k, i]
        return jnp.broadcast_to(rows[0:1, :], (128, tall)).T[:, 0:1]

    def inverse(i):
        return lax.rsqrt(total_col(0, i) / model + 1e-05)

    def square(here, i):
        x = states[here, :].astype(jnp.float32)
        sqs[0, i] = to_row(jnp.sum(x * x, axis=1, keepdims=True))

    def normalise(here, i):
        x = states[here, :].astype(jnp.float32)
        nrm[here, :] = (x * inverse(i) * gain[0:1, :]).astype(jnp.bfloat16)

    def wgrad(w, trans, factor):
        nblk, rows_per = part.shape[1], part.shape[2]

        def body(c, _):
            cols = pl.ds(pl.multiple_of(c * 256, 256), 256)
            out = jnp.dot(trans[...], factor[:, cols], preferred_element_type=jnp.float32)
            part[w, :, :, cols] = out.reshape(nblk, rows_per, 256)
            return 0

        lax.fori_loop(0, ncol, body, 0)

    def part_v(zz, h):
        return part[0, zz * 2 + h]

    def part_z(zz, h):
        return part[1, zz * 2 + h, half(1)]

    def part_o(zz, h):
        yo(zz, h).wait_recv()
        return part[1, zz * 2 + sq, half(h)] + yro[zz, h].astype(jnp.float32)

    def hops(d, h, buf_r, buf_l, s_r, r_r, s_l, r_l):
        for zz, valid, dev, fed, buf, ss, rs in (
            (dp + d, dp + d <= last, right, dp > 0, buf_r, s_r, r_r),
            (dp - d, dp - d >= 0, left, dp < last, buf_l, s_l, r_l),
        ):
            c = copy(buf.at[zz, h], buf.at[zz, h], ss.at[d - 1, h], rs.at[zz, h], dev)
            yield zz, valid, fed, buf, c

    def line_open(get, bufs, halves=(0, 1)):
        for d in range(last, 0, -1):
            for h in halves:
                for zz, valid, fed, buf, c in hops(d, h, *bufs):
                    opening = valid & jnp.logical_not(fed)

                    @pl.when(opening)
                    def _(zz=zz, h=h, buf=buf):
                        buf[zz, h] = get(zz, h).astype(jnp.bfloat16)

                    go(c, opening)

    def line(d, h, get, bufs):
        for zz, valid, fed, buf, c in hops(d, h, *bufs):

            @pl.when(valid & fed)
            def _(zz=zz, buf=buf, c=c):
                mine_part = get(zz, h)
                c.wait_recv()
                buf[zz, h] = (mine_part + buf[zz, h].astype(jnp.float32)).astype(jnp.bfloat16)

            go(c, valid & fed)

    def line_end(h, acc, bufs):
        buf_r, buf_l, s_r, r_r, s_l, r_l = bufs
        for fed, dev, buf, ss, rs in (
            (dp > 0, right, buf_r, s_r, r_r),
            (dp < last, left, buf_l, s_l, r_l),
        ):
            c = copy(buf.at[dp, h], buf.at[dp, h], ss.at[0, h], rs.at[dp, h], dev)

            @pl.when(fed)
            def _(c=c, buf=buf):
                c.wait_recv()
                acc[h] += buf[dp, h].astype(jnp.float32)

    line_v = (rbv, lbv, s_rv, r_rv, s_lv, r_lv)
    line_o = (rbo, lbo, s_ro, r_ro, s_lo, r_lo)
    line_z = (rbz, lbz, s_rz, r_rz, s_lz, r_lz)

    def yo(zz, h):
        return copy(yso.at[zz, h], yro.at[zz, h], s_yo.at[zz, h], r_yo.at[zz, h], ydev)

    def send_yo(zz, h, cond=None):
        def fill():
            yso[zz, h] = part[1, zz * 2 + (1 - sq), half(h)].astype(jnp.bfloat16)

        fill() if cond is None else pl.when(cond)(fill)
        go(yo(zz, h), cond)

    for h in range(2):
        ag_own_z(0, h)
        ag_own_y(0, h)
    for i in range(width // 128):
        gain[:, i * 128 : (i + 1) * 128] = jnp.broadcast_to(
            gain_in[i : i + 1, :].astype(jnp.float32), (8, 128)
        )
    local["states"].wait()
    row_loop(square)
    sq_copies = share(0)
    local["up"].wait()
    trans_v[...] = up[...].T

    first = starts[0:1, :] - sq * nbytes
    row8 = jnp.broadcast_to(first, (8, first.shape[1]))
    lane = lax.broadcasted_iota(jnp.int32, row8.shape, 1)
    after = jnp.where(
        lane == first.shape[1] - 1, 2 * nbytes, pltpu.roll(row8, first.shape[1] - 1, 1)
    )
    for w in range(first.shape[1] // WIN):
        lanes = slice(w * WIN, (w + 1) * WIN)
        bounds[w, 0:1, :] = first[:, lanes]
        bounds[w, 1:2, :] = after[0:1, lanes]
    bounds[first.shape[1] // WIN] = jnp.full(bounds.shape[1:], 4 * nbytes, jnp.int32)

    ag_forward(0, 1, 0)
    for h in range(2):
        ag_own_z(1, h, inner=False)
    for c in sq_copies:
        c.wait_recv()
    row_loop(normalise)
    ag_forward(0, 1, 1)
    wgrad(0, trans_v, nrm)
    line_open(part_v, line_v)
    ag_forward(0, 2, 0)
    nblocks = nbytes // BLK
    ends = lax.broadcasted_iota(jnp.int32, (nblocks, first.shape[1]), 0) * BLK + (BLK - 1)
    reach = (jnp.broadcast_to(first, ends.shape) <= ends).astype(jnp.int32)
    high = (jnp.sum(reach, axis=1, keepdims=True) - 1) // WIN
    low = (jnp.sum((first <= 0).astype(jnp.int32), axis=1, keepdims=True) - 1) // WIN
    step = lax.broadcasted_iota(jnp.int32, (nblocks, 128), 0) + high - low
    pair = lax.broadcasted_iota(jnp.int32, (nblocks, 128), 1)
    block_of = jnp.sum((step < pair).astype(jnp.int32), axis=0, keepdims=True)
    window = lax.broadcasted_iota(jnp.int32, (1, 128), 1) - block_of + low
    done = block_of >= nblocks
    tab[0:1, :] = jnp.where(done, nblocks - 1, block_of)
    nwin = first.shape[1] // WIN
    window = jnp.where(done, nwin, window)
    tab[1:2, :] = window
    window_of = jnp.broadcast_to(window.astype(jnp.float32), (128, 128)).T[: psums.shape[1], 0:1]
    local["tab"] = pltpu.make_async_copy(tab, tab_s, s_in.at[9])
    local["tab"].start()
    for w in range(nwin):
        bd[w, :WIN, HD:] = jnp.zeros((WIN, HD), jnp.bfloat16)
        bd[w, WIN:, :HD] = jnp.zeros((WIN, HD), jnp.bfloat16)
    bd[nwin] = jnp.zeros(bd.shape[1:], jnp.bfloat16)
    qb[nwin] = jnp.zeros((WIN, HD), jnp.bfloat16)
    gb[nwin] = jnp.zeros((WIN, HD), jnp.bfloat16)

    ag_forward(0, 2, 1)
    local["ctx"].wait()
    trans_o[...] = ctx[...].T
    for h in range(2):
        ag_forward(0, 3, h)
        ag_own_z(1, h, ends=False)
        ag_own_y(1, h)
    line(2, 0, part_v, line_v)
    ag_forward(1, 1, 0)
    local["vw"].wait()
    ag_wait_y(0)
    ag_forward(1, 1, 1)

    def project(here, i):
        full = wall[0].reshape(up.shape[1], width)
        g = jnp.dot(up[here, :], full, preferred_element_type=jnp.float32)
        gn[here, :] = g
        x = states[here, :].astype(jnp.float32)
        sqs[1, i] = to_row(jnp.sum(g * gain[0:1, :] * x, axis=1, keepdims=True))

    row_loop(project)
    cr_copies = share(1)
    line(2, 1, part_v, line_v)
    ag_cross(1, 0)
    ag_forward(1, 2, 0)
    ag_cross(1, 1)
    ag_forward(1, 2, 1)
    local["resid"].wait()
    for c in cr_copies:
        c.wait_recv()

    def make_grad(here, i):
        inv = inverse(i)
        cross = total_col(1, i) / model
        x = states[here, :].astype(jnp.float32)
        gpat[here, :] = (
            resid[here, :].astype(jnp.float32)
            + inv * gain[0:1, :] * gn[here, :]
            - (inv * inv * inv * cross) * x
        ).astype(jnp.bfloat16)

    row_loop(make_grad)
    ag_forward(1, 3, 0)
    ag_forward(1, 3, 1)
    local["q"].wait()
    qc = go(copy(qboth.at[sq], qboth.at[sq], s_g.at[0], r_g.at[0], ydev))
    wgrad(1, trans_o, gpat)
    line_open(part_z, line_z)
    for k in range(ndp - 1, 0, -1):
        send_yo(dp + k, 0, dp + k <= last)
        send_yo(dp - k, 0, dp - k >= 0)
    send_yo(dp, 0)
    for h in range(2):
        line(1, h, part_v, line_v)
    for h in range(2):
        line(2, h, part_z, line_z)
    local["ow"].wait()
    ag_wait_y(1)

    def tile(i):
        return pl.ds(i * tall, tall)

    def pa(i, k):
        return copy(gsend.at[k - 1, tile(i)], par.at[k - 1, tile(i)], s_pa.at[k - 1, i],
                    r_pa.at[k - 1, i], tdev(k))

    for i in range(nrow):
        full = wall[1].reshape(up.shape[1], width)
        p = lax.dot_general(
            gpat[tile(i), :], full, (((1,), (1,)), ((), ())), preferred_element_type=jnp.float32
        )
        for j in range(nt):
            pas[j, tile(i), :] = p[:, j * HD : (j + 1) * HD]
        for k in range(1, nt):
            gsend[k - 1, tile(i)] = pas[lax.rem(tn + k, nt), tile(i)].astype(jnp.bfloat16)
            go(pa(i, k))

    for h in range(2):
        acc[h] = part_v(dp, h)
        line_end(h, acc, line_v)
    ysv[...] = acc[1 - sq].astype(jnp.bfloat16)
    yv = go(copy(ysv, yrv, s_yv.at[0], r_yv.at[0], ydev))
    ngroup = psums.shape[1] // GROUP

    def e_copy(group):
        here = pl.ds(group * GROUP, GROUP)
        return pltpu.make_async_copy(expo.at[here], e_out.at[here], s_e.at[group])

    def p_copy(group):
        here = pl.ds(group * GROUP, GROUP)
        return pltpu.make_async_copy(pgrad.at[here], p_out.at[here], s_p.at[group])

    def scores(group, _):
        for k in range(GROUP):
            n = group * GROUP + k
            e = tile_scores(tab_s[0, n], tab_s[1, n], keys, qb, bounds).astype(jnp.bfloat16)
            expo[n] = e
            psums[0, pl.ds(n, 1), :] = jnp.sum(e.astype(jnp.float32), axis=0, keepdims=True)
        e_copy(group).start()
        return 0

    def products(group, _):
        for k in range(GROUP):
            n = group * GROUP + k
            pg = tile_products(tab_s[0, n], tab_s[1, n], values, gb)
            t = psums[0, pl.ds(n, 1), :]
            m = jnp.sum(expo[n].astype(jnp.float32) * pg, axis=0, keepdims=True)
            mean = m / jnp.where(t > 0.0, t, 1.0)
            pgrad[n] = (pg - mean).astype(jnp.bfloat16)
            psums[1, pl.ds(n, 1), :] = m
            means[pl.ds(n, 1), :] = mean
        p_copy(group).start()
        return 0

    def window_rows(w):
        return (w * WIN // patches, pl.ds(w * WIN % patches, WIN))

    def window_total(which, w):
        return jnp.sum(
            jnp.where(window_of == float(w), psums[which], 0.0), axis=0, keepdims=True
        )

    def open_scores():
        qc.wait_recv()
        for name in ("keys", "values", "tab"):
            local[name].wait()
        for w in range(nwin):
            rows = qboth[window_rows(w)]
            qb[w] = rows
            bd[w, :WIN, :HD] = rows

    def close_scores():
        for w in range(nwin):
            t = window_total(0, w)
            table[0:1, w * WIN : (w + 1) * WIN] = jnp.where(
                t > 0.0, 1.0 / jnp.where(t > 0.0, t, 1.0), 0.0
            )
        table[:, nwin * WIN :] = jnp.zeros((2, WIN), jnp.float32)

    open_scores()
    lax.fori_loop(0, ngroup, scores, 0)
    close_scores()
    line_open(part_o, line_o, (0,))
    for h in range(2):
        line(1, h, part_z, line_z)
    line(2, 0, part_o, line_o)
    gc = []
    for i in range(nrow):
        total = pas[tn, tile(i)]
        for k in range(1, nt):
            pa(i, k).wait_recv()
            total = total + par[k - 1, tile(i)].astype(jnp.float32)
        gboth[sq, tile(i)] = total.astype(jnp.bfloat16)
        block = gboth.at[sq, tile(i)]
        gc.append(go(copy(block, block, s_g.at[1 + i], r_g.at[1 + i], ydev)))
    for h in range(2):
        accz[h] = part_z(dp, h)
        line_end(h, accz, line_z)
    ysz[...] = accz[1 - sq].astype(jnp.bfloat16)
    yz = go(copy(ysz, yrz, s_yv.at[1], r_yv.at[1], ydev))
    line(1, 0, part_o, line_o)
    for c in gc:
        c.wait_recv()
    for w in range(nwin):
        rows = gboth[window_rows(w)]
        gb[w] = rows
        bd[w, WIN:, HD:] = rows
    out_bd = pltpu.make_async_copy(bd, bd_out, s_out.at[2])
    out_bd.start()
    lax.fori_loop(0, ngroup, products, 0)
    yv.wait_recv()
    acc[0] = acc[sq] + yrv[...].astype(jnp.float32)
    out_v = pltpu.make_async_copy(acc.at[0], wgv, s_out.at[0])
    out_v.start()
    for w in range(nwin):
        lanes = slice(w * WIN, (w + 1) * WIN)
        table[1:2, lanes] = window_total(1, w) * table[0:1, lanes]
    acco[0] = part_o(dp, 0)
    line_end(0, acco, line_o)
    yz.wait_recv()
    acco[1] = accz[sq] + yrz[...].astype(jnp.float32)
    out_o = pltpu.make_async_copy(acco, wgo, s_out.at[1])
    out_o.start()
    for group in range(ngroup):
        e_copy(group).wait()
        p_copy(group).wait()
    for c, cond in sent:
        if cond is None:
            c.wait_send()
        else:
            pl.when(cond)(c.wait_send)
    for c in (out_v, out_o, out_bd):
        c.wait()


def grad_call(ndp, nt, states, resid, up, gain, vw, ow, ctx, q, starts, keys, values):
    patches, width = states.shape
    rows = vw.shape[0]
    nblk = 2 * ndp
    nk = up.shape[1]
    bf, f32, i32 = jnp.bfloat16, jnp.float32, jnp.int32
    nrow = patches // 128
    nbytes = keys.shape[0] * BLK
    total = starts.shape[1]
    nwin = total // WIN
    npair = -(-(nbytes // BLK + nwin - 1) // GROUP) * GROUP
    vmem = pl.BlockSpec(memory_space=pltpu.VMEM)
    hbm = pl.BlockSpec(memory_space=pl.ANY)
    dma = pltpu.SemaphoreType.DMA
    return pl.pallas_call(
        functools.partial(grad_kernel, ndp, nt, nbytes),
        out_shape=(
            jax.ShapeDtypeStruct((rows, width), f32),
            jax.ShapeDtypeStruct((2, rows // 2, width), f32),
            jax.ShapeDtypeStruct((nwin + 1, 2 * WIN, 2 * HD), bf),
            jax.ShapeDtypeStruct((npair, BLK, WIN), bf),
            jax.ShapeDtypeStruct((npair, BLK, WIN), bf),
            jax.ShapeDtypeStruct((2, 128), i32),
            jax.ShapeDtypeStruct((2, total + WIN), f32),
            jax.ShapeDtypeStruct((npair, WIN), f32),
        ),
        in_specs=[hbm, hbm, hbm, vmem, hbm, hbm, hbm, hbm, vmem, hbm, hbm],
        out_specs=[hbm] * 5 + [vmem] * 3,
        scratch_shapes=[
            pltpu.VMEM((patches, width), bf),
            pltpu.VMEM((patches, width), bf),
            pltpu.VMEM((patches, nk), bf),
            pltpu.VMEM((patches, nk), bf),
            pltpu.VMEM((8, width), f32),
            pltpu.VMEM((2, nblk, rows, width), bf),
            pltpu.VMEM((2, nrow, 8, 128), f32),
            pltpu.VMEM((2, nt - 1, nrow, 8, 128), f32),
            pltpu.VMEM((2, nblk, rows, width), f32),
            pltpu.VMEM((2, rows, width), f32),
            pltpu.VMEM((2, rows // 2, width), f32),
            pltpu.VMEM((2, rows // 2, width), f32),
            pltpu.VMEM((ndp, 2, rows // 2, width), bf),
            pltpu.VMEM((ndp, 2, rows // 2, width), bf),
            pltpu.VMEM((rows // 2, width), bf),
            pltpu.VMEM((rows // 2, width), bf),
            pltpu.VMEM((ndp, 2, rows, width), bf),
            pltpu.VMEM((ndp, 2, rows, width), bf),
            pltpu.VMEM((rows, width), bf),
            pltpu.VMEM((rows, width), bf),
            pltpu.VMEM((ndp, 2, rows // 2, width), bf),
            pltpu.VMEM((ndp, 2, rows // 2, width), bf),
            pltpu.VMEM((ndp, 2, rows // 2, width), bf),
            pltpu.VMEM((ndp, 2, rows // 2, width), bf),
            pltpu.VMEM((nt, patches, HD), f32),
            pltpu.VMEM((nt - 1, patches, HD), bf),
            pltpu.VMEM((patches, width), f32),
            pltpu.VMEM((patches, width), bf),
            pltpu.VMEM((patches, width), bf),
            pltpu.VMEM((nk, patches), bf),
            pltpu.VMEM((nk, patches), bf),
            pltpu.VMEM((nt - 1, patches, HD), bf),
            pltpu.VMEM((2, patches, HD), bf),
            pltpu.VMEM((2, patches, HD), bf),
            pltpu.VMEM(keys.shape, bf),
            pltpu.VMEM(keys.shape, bf),
            pltpu.VMEM((nwin + 1, 2 * WIN, 2 * HD), bf),
            pltpu.VMEM((nwin + 1, WIN, HD), bf),
            pltpu.VMEM((nwin + 1, WIN, HD), bf),
            pltpu.VMEM((nwin + 1, 2, WIN), i32),
            pltpu.VMEM((npair, BLK, WIN), bf),
            pltpu.VMEM((npair, BLK, WIN), bf),
            pltpu.VMEM((2, npair, WIN), f32),
            pltpu.SMEM((2, 128), i32),
            dma((10,)), dma((npair // GROUP,)), dma((npair // GROUP,)), dma((3,)),
            dma((2, 2, 6 * ndp)), dma((2, 2, nblk)),
            dma((2, nt - 1)), dma((2, nt - 1)),
            dma((ndp, 2)), dma((ndp, 2)), dma((ndp, 2)), dma((ndp, 2)),
            dma((ndp, 2)), dma((ndp, 2)), dma((ndp, 2)), dma((ndp, 2)),
            dma((ndp, 2)), dma((ndp, 2)), dma((ndp, 2)), dma((ndp, 2)),
            dma((ndp, 2)), dma((ndp, 2)), dma((2,)), dma((2,)),
            dma((nt - 1, nrow)), dma((nt - 1, nrow)), dma((1 + nrow,)), dma((1 + nrow,)),
        ],
        compiler_params=pltpu.CompilerParams(
            collective_id=0, has_side_effects=True, vmem_limit_bytes=60 * 1024 * 1024
        ),
    )(states, resid, up, gain, vw, ow, ctx, q, starts, keys, values)


def byte_kernel(
    tab_in, table_in, means_in, bd_in, e_in, p_in, wgv_in, wgo_in, gk_out, gv_out, wgv, wgo,
    tab, table, means, bd, expo, pgrad, gk, gv, held, s_e, s_p, o_k, o_v, s_w, s_t,
):
    nwin = bd.shape[0] - 1
    nbytes = gk.shape[0]
    ngroup = expo.shape[0] // GROUP
    nchunk = o_k.shape[0]
    chunk = nbytes // nchunk
    ready = GROUP * BLK // chunk
    behind = -(-(nwin - 1) // (chunk // BLK))
    scale = 1.0 / math.sqrt(HD)

    def load(c):
        here = pl.ds(c * GROUP, GROUP)
        return (
            pltpu.make_async_copy(e_in.at[here], expo.at[here], s_e.at[c]),
            pltpu.make_async_copy(p_in.at[here], pgrad.at[here], s_p.at[c]),
        )

    def store(c):
        here = pl.ds(pl.multiple_of(c * chunk, chunk), chunk)
        return (
            pltpu.make_async_copy(gk.at[here], gk_out.at[here], o_k.at[c]),
            pltpu.make_async_copy(gv.at[here], gv_out.at[here], o_v.at[c]),
        )

    small = [
        pltpu.make_async_copy(a, b, s_t.at[i])
        for i, (a, b) in enumerate((
            (tab_in, tab), (table_in, table), (means_in, means), (bd_in, bd)
        ))
    ]
    for x in small:
        x.start()
    for c in range(ngroup):
        for x in load(c):
            x.start()
    carried = ((wgv_in, wgv), (wgo_in, wgo))
    taken = [pltpu.make_async_copy(a, held.at[i], s_w.at[i]) for i, (a, _) in enumerate(carried)]
    passed = [pltpu.make_async_copy(held.at[i], b, s_w.at[2 + i]) for i, (_, b) in enumerate(carried)]
    for x in taken:
        x.start()
    for x in small:
        x.wait()

    def apply(group, _):
        for x in load(group):
            x.wait()
        first = group * GROUP
        prior = jnp.maximum(first - 1, 0)
        before = pl.ds(pl.multiple_of(tab[0, prior] * BLK, BLK), BLK)
        held_k, held_v = gk[before, :], gv[before, :]
        for k in range(GROUP):
            n = first + k
            b, w = tab[0, n], tab[1, n]
            here = pl.ds(pl.multiple_of(b * BLK, BLK), BLK)
            lanes = pl.ds(pl.multiple_of(w * WIN, WIN), WIN)
            same = tab[0, jnp.maximum(n - 1, 0)] == b
            same = same & (n > 0) if k == 0 else same
            p = expo[n].astype(jnp.float32) * table[0:1, lanes]
            shift = means[pl.ds(n, 1), :] - table[1:2, lanes]
            sg = p * (pgrad[n].astype(jnp.float32) + shift) * scale
            both = jnp.concatenate([sg.astype(jnp.bfloat16), p.astype(jnp.bfloat16)], axis=1)
            out = jnp.dot(both, bd[w], preferred_element_type=jnp.float32).astype(jnp.bfloat16)
            held_k = out[:, :HD] + jnp.where(same, held_k, jnp.zeros_like(held_k))
            held_v = out[:, HD:] + jnp.where(same, held_v, jnp.zeros_like(held_v))
            gk[here, :] = held_k
            gv[here, :] = held_v

        for r in range(ready):
            done = group * ready + r - behind

            @pl.when((done >= 0) & (done < nchunk))
            def _(done=done):
                for x in store(done):
                    x.start()

        return 0

    lax.fori_loop(0, 1, apply, 0)
    for x, y in zip(taken, passed):
        x.wait()
        y.start()
    lax.fori_loop(1, ngroup, apply, 0)
    for c in range(max(ngroup * ready - behind, 0), nchunk):
        for x in store(c):
            x.start()
    for c in range(nchunk):
        for x in store(c):
            x.wait()
    for x in passed:
        x.wait()


def byte_call(tab, table, means, bd, expo, pgrad, wgv, wgo, out):
    bf, f32 = jnp.bfloat16, jnp.float32
    nchunk = out.shape[0] // 2048
    ngroup = expo.shape[0] // GROUP
    hbm = pl.BlockSpec(memory_space=pl.ANY)
    dma = pltpu.SemaphoreType.DMA
    return pl.pallas_call(
        byte_kernel,
        out_shape=(
            out,
            out,
            jax.ShapeDtypeStruct(wgv.shape, f32),
            jax.ShapeDtypeStruct(wgo.shape, f32),
        ),
        in_specs=[hbm] * 8,
        out_specs=[hbm] * 4,
        scratch_shapes=[
            pltpu.SMEM(tab.shape, jnp.int32), pltpu.VMEM(table.shape, f32),
            pltpu.VMEM(means.shape, f32), pltpu.VMEM(bd.shape, bf), pltpu.VMEM(expo.shape, bf), pltpu.VMEM(pgrad.shape, bf),
            pltpu.VMEM(out.shape, bf), pltpu.VMEM(out.shape, bf),
            pltpu.VMEM((2,) + wgv.shape, f32),
            dma((ngroup,)), dma((ngroup,)), dma((nchunk,)), dma((nchunk,)), dma((4,)), dma((4,)),
        ],
        compiler_params=pltpu.CompilerParams(vmem_limit_bytes=60 * 1024 * 1024),
    )(tab, table, means, bd, expo, pgrad, wgv, wgo)


def on_device_kernels(
    ndp, nt, patch_states, residual_grad, upstream_value, norm_gain, value_weight, out_weight,
    attn_out, queries, byte_keys, byte_values, patch_starts,
):
    wgv, wgo, bd, expo, pgrad, tab, table, means = grad_call(
        ndp, nt, patch_states[0], residual_grad[0], upstream_value[0],
        norm_gain.reshape(-1, 128), value_weight, out_weight, attn_out[0], queries[0], patch_starts,
        byte_keys.reshape(-1, BLK, HD), byte_values.reshape(-1, BLK, HD),
    )
    gk, gv, wgv, wgo = byte_call(
        tab, table, means, bd, expo, pgrad, wgv, wgo.reshape(wgv.shape),
        jax.ShapeDtypeStruct(byte_keys[0].shape, jnp.bfloat16),
    )
    return (wgv, wgo, gk[None], gv[None])


def solution(mesh):
    ndp, nseq, nt = mesh.shape["dp"], mesh.shape["seq"], mesh.shape["tensor"]
    use_kernels = nseq == 2 and ndp == 4
    body = functools.partial(on_device_kernels, ndp, nt) if use_kernels else on_device
    return jax.shard_map(
        body,
        mesh=mesh,
        in_specs=(
            P("dp", "seq", "tensor"),
            P("dp", "seq", "tensor"),
            P("dp", "seq", None),
            P("tensor"),
            P(("dp", "seq"), "tensor"),
            P(("dp", "seq"), "tensor"),
            P("dp", "seq", None),
            P("dp", "seq", "tensor"),
            P("dp", "seq", "tensor"),
            P("dp", "seq", "tensor"),
            P("dp", None),
        ),
        out_specs=(
            P(("dp", "seq"), "tensor"),
            P(("dp", "seq"), "tensor"),
            P("dp", "seq", "tensor"),
            P("dp", "seq", "tensor"),
        ),
        check_vma=False,
    )
```
